256 devices in a mesh: leaf: 32 (over y, x, core), front: 8 (over z).
Axes of the slice: x: 4, y: 4, z: 8, core: 2. Of those that a mesh axis runs over, the one named last changes fastest.
Arguments:
- leaf_contrib: float32 [32768, 1024], P(('leaf', 'front')), may hold values from -1 to 7, as said below
- entries_lower: float32 [32768, 1024], P(('leaf', 'front')), may hold values from -1 to 4, as said below
- entries_middle: float32 [16384, 1024], P(('leaf', 'front')), may hold values from -1 to 4, as said below
- entries_upper: float32 [8192, 1024], P(('leaf', 'front')), may hold values from -1 to 4, as said below
- assembly_lower: int32 [16, 2, 8], replicated, may hold values from 0 to 15, as said below
- assembly_middle: int32 [8, 2, 8], replicated, may hold values from 0 to 15, as said below
- assembly_upper: int32 [4, 2, 8], replicated, may hold values from 0 to 15, as said below
Outputs:
- factor_lower: float32 [32768, 1024], P(('leaf', 'front'))
- factor_middle: float32 [16384, 1024], P(('leaf', 'front'))
- factor_upper: float32 [8192, 1024], P(('leaf', 'front'))
- top_update: float32 [4096, 1024], P(('leaf', 'front'))
The draws below stay inside these ranges and needn't reach their ends.
Inputs may be any that keep to these rules, and one draw needn't show every extreme that they name: `leaf_contrib`: in natural row order each leaf's block is symmetric positive definite. `entries_lower`: in natural row order the first 1024 rows of each front's entries form a symmetric positive definite block. `entries_middle`: in natural row order the first 1024 rows of each front's entries form a symmetric positive definite block. `entries_upper`: in natural row order the first 1024 rows of each front's entries form a symmetric positive definite block. `assembly_lower`: each child's block j goes to parent block j or j + 8, and at least one of the two children sends its block j to j + 8. `assembly_middle`: each child's block j goes to parent block j or j + 8, and at least one of the two children sends its block j to j + 8. `assembly_upper`: each child's block j goes to parent block j or j + 8, and at least one of the two children sends its block j to j + 8.
All inputs are finite; a program needn't handle non-finite values.
Results may differ from the reference program's by a relative error of at most 0.0003.
Values sent between devices are 32-bit elements; how exact they have to be, the bound alone decides.
A program may use at most 128 MiB of HBM per device.

```python
import math
import jax
import jax.numpy as jnp
import numpy as np
from jax import lax

BLK = 128
PIVOT_BLOCKS = 8
LEVELS = 3
PIVOT = 1024
FRONT = 2048
LOCAL_BLOCKS = 1
FRONTS_LOWER = 16
FRONTS_MIDDLE = 8
FRONTS_UPPER = 4
N_LEAF = 32


def bit_reverse_drawn(number, bit_count):
    result = 0
    for bit_index in range(bit_count):
        result = result | (number >> bit_index & 1) << bit_count - 1 - bit_index
    return result


def stored_rows(height, update_only):
    groups = 2 ** height
    piece_rows = BLK // groups
    front_devs = PIVOT_BLOCKS // LOCAL_BLOCKS
    portions = (1,) if update_only else (0, 1)
    row_list = []
    for member in range(groups):
        for front_dev in range(front_devs):
            for portion in portions:
                for local_block in range(LOCAL_BLOCKS):
                    block_index = front_dev + front_devs * local_block
                    if not update_only:
                        block_index = block_index + portion * PIVOT_BLOCKS
                    first_row = block_index * BLK + bit_reverse_drawn(member, height) * piece_rows
                    row_list.extend(range(first_row, first_row + piece_rows))
    return np.array(row_list, dtype=np.int32)


def symmetric_noise(noise_key, count, order_size):
    noise = jax.random.uniform(noise_key, (count, order_size, order_size), jnp.float32, -1.0, 1.0)
    return (noise + jnp.swapaxes(noise, 1, 2)) * (0.5 / math.sqrt(order_size))


def coupling_term(coupling_key, count, order_size):
    vector = jax.random.uniform(coupling_key, (count, order_size), jnp.float32, 0.0, 1.0)
    return 0.5 * vector[:, :, None] * vector[:, None, :]


def draw_leaf_contrib(key, part):
    key = jax.random.fold_in(key, 7)
    noise_key = jax.random.fold_in(key, 0)
    diag_key = jax.random.fold_in(key, 1)
    coupling_key = jax.random.fold_in(key, 3)
    matrix = symmetric_noise(noise_key, N_LEAF, PIVOT)
    diagonal = jax.random.uniform(diag_key, (N_LEAF, PIVOT), jnp.float32, 3.0, 4.5)
    matrix = matrix + diagonal[:, :, None] * jnp.eye(PIVOT, dtype=jnp.float32)[None]
    matrix = matrix + coupling_term(coupling_key, N_LEAF, PIVOT)
    return matrix[:, stored_rows(0, True)].reshape(N_LEAF * PIVOT, PIVOT)


def entries_draw(key, fronts, height):
    noise_key = jax.random.fold_in(key, 0)
    diag_key = jax.random.fold_in(key, 1)
    lower_key = jax.random.fold_in(key, 2)
    coupling_key = jax.random.fold_in(key, 4)
    pivot_part = symmetric_noise(noise_key, fronts, PIVOT)
    spread = jax.random.uniform(diag_key, (fronts, PIVOT), jnp.float32, 0.0, 1.0)
    diagonal = 1.3 + 1.3 * spread
    pivot_part = pivot_part + diagonal[:, :, None] * jnp.eye(PIVOT, dtype=jnp.float32)[None]
    pivot_part = pivot_part + coupling_term(coupling_key, fronts, PIVOT)
    update_part = jax.random.uniform(lower_key, (fronts, PIVOT, PIVOT), jnp.float32, -1.0, 1.0) * (0.55 / math.sqrt(PIVOT))
    matrix = jnp.concatenate([pivot_part, update_part], axis=1)
    return matrix[:, stored_rows(height, False)].reshape(fronts * FRONT, PIVOT)


def draw_entries_lower(key, part):
    return entries_draw(jax.random.fold_in(key, 11), FRONTS_LOWER, 1)


def draw_entries_middle(key, part):
    return entries_draw(jax.random.fold_in(key, 12), FRONTS_MIDDLE, 2)


def draw_entries_upper(key, part):
    return entries_draw(jax.random.fold_in(key, 13), FRONTS_UPPER, 3)


def assembly_draw(key, fronts):
    choice_key, force_key = jax.random.split(key)
    selection = jax.random.randint(choice_key, (fronts, PIVOT_BLOCKS), 0, 3, dtype=jnp.int32)
    forced = 1 + jax.random.randint(force_key, (fronts, PIVOT_BLOCKS), 0, 2, dtype=jnp.int32)
    first_cell = (jnp.arange(fronts)[:, None] == 0) & (jnp.arange(PIVOT_BLOCKS)[None, :] == 0)
    selection = jnp.where(first_cell, forced, selection)
    blocks = jnp.arange(PIVOT_BLOCKS, dtype=jnp.int32)[None, :]
    first_child = blocks + PIVOT_BLOCKS * (selection != 1).astype(jnp.int32)
    second_child = blocks + PIVOT_BLOCKS * (selection != 2).astype(jnp.int32)
    return jnp.stack([first_child, second_child], axis=1).astype(jnp.int32)


def draw_assembly_lower(key, part):
    return assembly_draw(jax.random.fold_in(key, 21), FRONTS_LOWER)


def draw_assembly_middle(key, part):
    return assembly_draw(jax.random.fold_in(key, 22), FRONTS_MIDDLE)


def draw_assembly_upper(key, part):
    return assembly_draw(jax.random.fold_in(key, 23), FRONTS_UPPER)


def setup_inputs(seed: int = 0) -> dict:
    key_list = jax.random.split(jax.random.key(seed), 8)
    leaf_contrib = draw_leaf_contrib(jax.random.fold_in(key_list[7], 71), 0)
    entries_lower = draw_entries_lower(jax.random.fold_in(key_list[7], 71), 0)
    entries_middle = draw_entries_middle(jax.random.fold_in(key_list[7], 71), 0)
    entries_upper = draw_entries_upper(jax.random.fold_in(key_list[7], 71), 0)
    assembly_lower = draw_assembly_lower(jax.random.fold_in(key_list[7], 71), 0)
    assembly_middle = draw_assembly_middle(jax.random.fold_in(key_list[7], 71), 0)
    assembly_upper = draw_assembly_upper(jax.random.fold_in(key_list[7], 71), 0)
    return dict(leaf_contrib=leaf_contrib, entries_lower=entries_lower, entries_middle=entries_middle, entries_upper=entries_upper, assembly_lower=assembly_lower, assembly_middle=assembly_middle, assembly_upper=assembly_upper)


def bit_reverse(number, bit_count):
    result = 0
    for bit_index in range(bit_count):
        result = result | (number >> bit_index & 1) << bit_count - 1 - bit_index
    return result

def natural_rows(height, update_only):
    groups = 2 ** height
    piece_rows = BLK // groups
    front_devs = PIVOT_BLOCKS // LOCAL_BLOCKS
    portions = (1,) if update_only else (0, 1)
    row_list = []
    for member in range(groups):
        for front_dev in range(front_devs):
            for portion in portions:
                for local_block in range(LOCAL_BLOCKS):
                    block_index = front_dev + front_devs * local_block
                    if not update_only:
                        block_index = block_index + portion * PIVOT_BLOCKS
                    first_row = block_index * BLK + bit_reverse(member, height) * piece_rows
                    row_list.extend(range(first_row, first_row + piece_rows))
    return np.array(row_list, dtype=np.int32)

def assemble(entries, first_child, second_child, routes):
    matrix = jnp.zeros((FRONT, FRONT), jnp.float32)
    matrix = matrix.at[:, :PIVOT].set(entries)
    matrix = matrix.at[:PIVOT, PIVOT:].set(entries[PIVOT:].T)
    offsets = jnp.arange(BLK, dtype=jnp.int32)
    for child_index, child_block in ((0, first_child), (1, second_child)):
        places = (routes[child_index][:, None] * BLK + offsets[None, :]).reshape(-1).astype(jnp.int32)
        matrix = matrix.at[places[:, None], places[None, :]].add(child_block)
    return matrix

def factor_front(operands):
    entries, first_child, second_child, routes = operands
    matrix = assemble(entries, first_child, second_child, routes)
    lower_factor = jnp.linalg.cholesky(matrix[:PIVOT, :PIVOT])
    panel_rows = jax.scipy.linalg.solve_triangular(lower_factor, matrix[PIVOT:, :PIVOT].T, lower=True).T
    schur_block = matrix[PIVOT:, PIVOT:] - jnp.dot(panel_rows.astype(jnp.float32), panel_rows.T.astype(jnp.float32), precision=lax.Precision.HIGHEST, preferred_element_type=jnp.float32)
    return (jnp.concatenate([lower_factor, panel_rows], axis=0), schur_block)

def reference(leaf_contrib, entries_lower, entries_middle, entries_upper, assembly_lower, assembly_middle, assembly_upper):
    leaf_order = natural_rows(0, True)
    contrib = leaf_contrib.reshape(N_LEAF, PIVOT, PIVOT)[:, np.argsort(leaf_order)]
    outputs = []
    for height, entries, routes in ((1, entries_lower, assembly_lower), (2, entries_middle, assembly_middle), (3, entries_upper, assembly_upper)):
        fronts = N_LEAF // 2 ** height
        row_order = natural_rows(height, False)
        natural_entries = entries.reshape(fronts, FRONT, PIVOT)[:, np.argsort(row_order)]
        children = contrib.reshape(fronts, 2, PIVOT, PIVOT)
        factors, contrib = lax.map(factor_front, (natural_entries, children[:, 0], children[:, 1], routes))
        outputs.append(factors[:, row_order].reshape(fronts * FRONT, PIVOT))
    top_order = natural_rows(LEVELS, True)
    top_update = contrib[:, top_order].reshape(-1, PIVOT)
    return (outputs[0], outputs[1], outputs[2], top_update)
```

```python
import functools

import jax
import jax.numpy as jnp
from jax import lax
from jax.experimental import pallas as pl
from jax.experimental.pallas import tpu as pltpu
from jax.sharding import PartitionSpec as P

BLK = 128
PIVOT_BLOCKS = 8


def partner_2(value, axis, stride):
    mask = 2**stride
    pairs = [(source, source ^ mask) for source in range(lax.axis_size(axis))]
    return lax.ppermute(value, axis, pairs)


def product(left, right):
    return jnp.dot(left, right, precision=lax.Precision.HIGHEST, preferred_element_type=jnp.float32)


SB = 16

def split(x):
    h = x.astype(jnp.bfloat16)
    return h, (x - h.astype(jnp.float32)).astype(jnp.bfloat16)

def dotb(a, b):
    return jnp.dot(a, b, preferred_element_type=jnp.float32)

def dott(a, b):
    return lax.dot_general(a, b, (((1,), (1,)), ((), ())), preferred_element_type=jnp.float32)

def substep(g_ref, u_ref, s):
    base = s * SB
    p = g_ref[base:base + SB, :]
    cols = [jnp.broadcast_to(p[:, base + k:base + k + 1], (SB, 128)) for k in range(SB)]
    pl_, pr_ = p[:, :128], p[:, 128:]
    sub = lax.broadcasted_iota(jnp.int32, (SB, 128), 0)
    ul = jnp.zeros((SB, 128), jnp.float32)
    ur = jnp.zeros((SB, 128), jnp.float32)
    for r in range(SB):
        hit = sub == r
        v = cols[r]
        piv = jnp.broadcast_to(v[r:r + 1], (SB, 128))
        rs = lax.rsqrt(piv)
        inv = rs * rs
        rl = jnp.broadcast_to(pl_[r:r + 1], (SB, 128))
        rr = jnp.broadcast_to(pr_[r:r + 1], (SB, 128))
        ul = jnp.where(hit, rl * rs, ul)
        ur = jnp.where(hit, rr * rs, ur)
        vi = jnp.where(hit, 0.0, v * inv)
        for k in range(r + 1, SB):
            c = jnp.broadcast_to(cols[k][r:r + 1], (SB, 128))
            cols[k] = jnp.where(hit, c * inv, cols[k] - vi * c)
        pl_ = jnp.where(hit, rl * inv, pl_ - vi * rl)
        pr_ = jnp.where(hit, rr * inv, pr_ - vi * rr)
    u_ref[base:base + SB, :128] = ul
    u_ref[base:base + SB, 128:] = ur
    if s < 128 // SB - 1:
        lo = base + SB
        R = jnp.concatenate([pl_, pr_], 1)
        rh, rlo = split(R)
        parts = []
        def pad(x):
            z = []
            if base: z.append(jnp.zeros((base, 256), jnp.bfloat16))
            z.append(x)
            if 128 - lo: z.append(jnp.zeros((128 - lo, 256), jnp.bfloat16))
            return jnp.concatenate(z, 0)
        d = g_ref[lo:, :128]
        dh, dl = split(d)
        upd = dotb(jnp.concatenate([dh, dl], 1), jnp.concatenate([pad(rh), pad(rh)], 0)) + dotb(dh, pad(rlo))
        g_ref[lo:, :] = g_ref[lo:, :] - upd

def kernel(m, a_ref, b_ref, l_ref, x_ref, xh, xl, col, g_ref, u_ref):
    n = 8
    lane = lax.broadcasted_iota(jnp.int32, (128, 128), 1)
    row = lax.broadcasted_iota(jnp.int32, (128, 128), 0)
    def step(k, _):
        for kk in range(n):
            @pl.when(k == kk)
            def _():
                rows = 1024 - kk * 128
                c = jnp.concatenate([a_ref[kk * 128:, kk * 128:(kk + 1) * 128], b_ref[:, kk * 128:(kk + 1) * 128]], 0)
                if kk:
                    K = kk * 128
                    rh, rl = xh[kk * 128:(kk + 1) * 128, :K], xl[kk * 128:(kk + 1) * 128, :K]
                    c = c - (dott(xh[kk * 128:, :K], rh) + (dott(xh[kk * 128:, :K], rl) + dott(xl[kk * 128:, :K], rh)))
                g_ref[:, :128] = c[:128]
                col[kk * 128 + 128:, :] = c[128:]
        g_ref[:, 128:] = jnp.where(lane == row, 1.0, 0.0)
        for s in range(128 // SB):
            substep(g_ref, u_ref, s)
        k128 = pl.multiple_of(k * 128, 128)
        l_ref[pl.ds(k128, 128), pl.ds(k128, 128)] = jnp.where(lane <= row, u_ref[:, :128].T, 0.0)
        wh, wl = split(u_ref[:, 128:])
        for kk in range(n):
            @pl.when(k == kk)
            def _():
                ch, cl = split(col[kk * 128 + 128:, :])
                x = dott(ch, wh) + (dott(ch, wl) + dott(cl, wh))
                if kk < n - 1:
                    l_ref[kk * 128 + 128:, kk * 128:(kk + 1) * 128] = x[:1024 - kk * 128 - 128]
                    l_ref[:kk * 128 + 128, (kk + 1) * 128:(kk + 2) * 128] = jnp.zeros((kk * 128 + 128, 128), jnp.float32)
                x_ref[:, kk * 128:(kk + 1) * 128] = x[1024 - kk * 128 - 128:]
                h, l = split(x)
                xh[kk * 128 + 128:, kk * 128:(kk + 1) * 128] = h
                xl[kk * 128 + 128:, kk * 128:(kk + 1) * 128] = l
        return 0
    lax.fori_loop(0, n, step, 0)

def factor_panel(a, b):
    m = b.shape[0]
    vm = pl.BlockSpec(memory_space=pltpu.VMEM)
    return pl.pallas_call(
        functools.partial(kernel, m),
        out_shape=(jax.ShapeDtypeStruct((1024, 1024), jnp.float32), jax.ShapeDtypeStruct((m, 1024), jnp.float32)),
        in_specs=[vm, vm], out_specs=(vm, vm),
        scratch_shapes=[pltpu.VMEM((1024 + m, 1024), jnp.bfloat16), pltpu.VMEM((1024 + m, 1024), jnp.bfloat16),
                        pltpu.VMEM((1024 + m, 128), jnp.float32), pltpu.VMEM((128, 256), jnp.float32), pltpu.VMEM((128, 256), jnp.float32)],
        compiler_params=pltpu.CompilerParams(vmem_limit_bytes=60 * 2**20),
        name="factor_panel",
    )(a, b)


def reversed_bits(number, bit_count):
    result = jnp.zeros((), jnp.int32)
    for bit_index in range(bit_count):
        result = result + (number >> bit_index & 1) * (1 << bit_count - 1 - bit_index)
    return result


def join_pieces(mine, theirs, bit_index, axis_index):
    upper_bit = lax.axis_index("leaf") >> bit_index & 1
    return jnp.where(
        upper_bit == 0,
        jnp.concatenate([mine, theirs], axis_index),
        jnp.concatenate([theirs, mine], axis_index),
    )


def group_gather(pieces, height):
    gathered = lax.all_gather(pieces[:, None], "front", axis=1, tiled=True)
    for bit_index in reversed(range(height)):
        partner = partner_2(gathered, "leaf", bit_index)
        gathered = join_pieces(gathered, partner, bit_index, 2)
    return gathered


def spread_columns(rows_in, upper_mask):
    blocks = rows_in.reshape(rows_in.shape[0], rows_in.shape[1], upper_mask.shape[0], -1)
    to_pivot = blocks * (1.0 - upper_mask)[None, None, :, None]
    to_update = blocks * upper_mask[None, None, :, None]
    return jnp.concatenate([to_pivot, to_update], axis=2).reshape(
        rows_in.shape[0], rows_in.shape[1], -1
    )


def own_rows(whole, front_index, piece_index, piece_rows):
    chosen = lax.dynamic_index_in_dim(whole, front_index, 1, keepdims=False)
    return lax.dynamic_slice_in_dim(chosen, piece_index * piece_rows, piece_rows, 1)


def local(
    leaf_contrib,
    entries_lower,
    entries_middle,
    entries_upper,
    assembly_lower,
    assembly_middle,
    assembly_upper,
):
    front_count = lax.axis_size("front")
    local_count = PIVOT_BLOCKS // front_count
    leaf_index = lax.axis_index("leaf")
    front_index = lax.axis_index("front")
    pivot_size = leaf_contrib.shape[1]
    update = leaf_contrib.reshape(local_count, BLK, pivot_size)
    my_blocks = front_index + front_count * jnp.arange(local_count, dtype=jnp.int32)
    selector = (jnp.arange(PIVOT_BLOCKS, dtype=jnp.int32)[None, :] == my_blocks[:, None]).astype(
        jnp.float32
    )
    results = []
    for height, entries, routes in (
        (1, entries_lower, assembly_lower),
        (2, entries_middle, assembly_middle),
        (3, entries_upper, assembly_upper),
    ):
        piece_rows = BLK // 2**height
        child_bit = leaf_index >> height - 1 & 1
        low_rows = update[:, :piece_rows]
        high_rows = update[:, piece_rows:]
        kept = jnp.where(child_bit == 0, low_rows, high_rows)
        outgoing = jnp.where(child_bit == 0, high_rows, low_rows)
        received = partner_2(outgoing, "leaf", height - 1)
        route_pair = lax.dynamic_index_in_dim(routes, leaf_index >> height, 0, keepdims=False)
        upper_masks = (route_pair >= PIVOT_BLOCKS).astype(jnp.float32)
        own_mask = jnp.where(child_bit == 0, upper_masks[0], upper_masks[1])
        other_mask = jnp.where(child_bit == 0, upper_masks[1], upper_masks[0])
        slab_rows = local_count * piece_rows
        pivot_slab = entries[:slab_rows].reshape(local_count, piece_rows, pivot_size)
        update_slab = jnp.zeros((local_count, piece_rows, 2 * pivot_size), jnp.float32)
        update_slab = update_slab.at[:, :, :pivot_size].set(
            entries[slab_rows:].reshape(local_count, piece_rows, pivot_size)
        )
        for contribution, column_mask in ((kept, own_mask), (received, other_mask)):
            spread = spread_columns(contribution, column_mask)
            row_upper = jnp.sum(selector * column_mask[None, :], axis=1)
            pivot_slab = pivot_slab + (1.0 - row_upper)[:, None, None] * spread[:, :, :pivot_size]
            update_slab = update_slab + row_upper[:, None, None] * spread
        piece_index = reversed_bits(leaf_index & 2**height - 1, height)
        update_pivot = update_slab[:, :, :pivot_size]
        whole_pivot = group_gather(pivot_slab, height).reshape(pivot_size, pivot_size)
        lower_factor, own_panel = factor_panel(whole_pivot, update_pivot.reshape(-1, pivot_size))
        all_panel = group_gather(
            own_panel.reshape(local_count, piece_rows, pivot_size), height
        ).reshape(pivot_size, pivot_size)
        own_factor = own_rows(
            lower_factor.reshape(local_count, front_count, BLK, pivot_size),
            front_index,
            piece_index,
            piece_rows,
        ).reshape(-1, pivot_size)
        results.append(jnp.concatenate([own_factor, own_panel], axis=0))
        schur_rows = update_slab[:, :, pivot_size:].reshape(-1, pivot_size) - product(
            own_panel, all_panel.T
        )
        update = schur_rows.reshape(local_count, piece_rows, pivot_size)
    return (results[0], results[1], results[2], update.reshape(-1, pivot_size))


def solution(mesh):
    in_specs = (
        P(("leaf", "front"), None),
        P(("leaf", "front"), None),
        P(("leaf", "front"), None),
        P(("leaf", "front"), None),
        P(),
        P(),
        P(),
    )
    out_specs = (
        P(("leaf", "front"), None),
        P(("leaf", "front"), None),
        P(("leaf", "front"), None),
        P(("leaf", "front"), None),
    )
    return jax.shard_map(local, mesh=mesh, in_specs=in_specs, out_specs=out_specs, check_vma=False)
```

```python
import functools

import jax
import jax.numpy as jnp
from jax import lax
from jax.experimental import pallas as pl
from jax.experimental.pallas import tpu as pltpu
from jax.sharding import PartitionSpec as P

BLK = 128
SB = 16

def split(x):
    h = x.astype(jnp.bfloat16)
    return h, (x - h.astype(jnp.float32)).astype(jnp.bfloat16)

def dotb(a, b):
    return jnp.dot(a, b, preferred_element_type=jnp.float32)

def dott(a, b):
    return lax.dot_general(a, b, (((1,), (1,)), ((), ())), preferred_element_type=jnp.float32)

def substep(g_ref, u_ref, s):
    base = s * SB
    p = g_ref[base:base + SB, :]
    cols = [jnp.broadcast_to(p[:, base + k:base + k + 1], (SB, 128)) for k in range(SB)]
    pl_, pr_ = p[:, :128], p[:, 128:]
    sub = lax.broadcasted_iota(jnp.int32, (SB, 128), 0)
    ul = jnp.zeros((SB, 128), jnp.float32)
    ur = jnp.zeros((SB, 128), jnp.float32)
    for r in range(SB):
        hit = sub == r
        v = cols[r]
        piv = jnp.broadcast_to(v[r:r + 1], (SB, 128))
        rs = lax.rsqrt(piv)
        inv = rs * rs
        rl = jnp.broadcast_to(pl_[r:r + 1], (SB, 128))
        rr = jnp.broadcast_to(pr_[r:r + 1], (SB, 128))
        ul = jnp.where(hit, rl * rs, ul)
        ur = jnp.where(hit, rr * rs, ur)
        vi = jnp.where(hit, 0.0, v * inv)
        for k in range(r + 1, SB):
            c = jnp.broadcast_to(cols[k][r:r + 1], (SB, 128))
            cols[k] = jnp.where(hit, c * inv, cols[k] - vi * c)
        pl_ = jnp.where(hit, rl * inv, pl_ - vi * rl)
        pr_ = jnp.where(hit, rr * inv, pr_ - vi * rr)
    u_ref[base:base + SB, :128] = ul
    u_ref[base:base + SB, 128:] = ur
    if s < 128 // SB - 1:
        lo = base + SB
        R = jnp.concatenate([pl_, pr_], 1)
        rh, rlo = split(R)
        parts = []
        def pad(x):
            z = []
            if base: z.append(jnp.zeros((base, 256), jnp.bfloat16))
            z.append(x)
            if 128 - lo: z.append(jnp.zeros((128 - lo, 256), jnp.bfloat16))
            return jnp.concatenate(z, 0)
        d = g_ref[lo:, :128]
        dh, dl = split(d)
        upd = dotb(jnp.concatenate([dh, dl], 1), jnp.concatenate([pad(rh), pad(rh)], 0)) + dotb(dh, pad(rlo))
        g_ref[lo:, :] = g_ref[lo:, :] - upd

def kernel(m, a_ref, b_ref, l_ref, x_ref, xh, xl, col, g_ref, u_ref):
    n = 8
    lane = lax.broadcasted_iota(jnp.int32, (128, 128), 1)
    row = lax.broadcasted_iota(jnp.int32, (128, 128), 0)
    def step(k, _):
        for kk in range(n):
            @pl.when(k == kk)
            def _():
                rows = 1024 - kk * 128
                c = jnp.concatenate([a_ref[kk * 128:, kk * 128:(kk + 1) * 128], b_ref[:, kk * 128:(kk + 1) * 128]], 0)
                if kk:
                    K = kk * 128
                    rh, rl = xh[kk * 128:(kk + 1) * 128, :K], xl[kk * 128:(kk + 1) * 128, :K]
                    c = c - (dott(xh[kk * 128:, :K], rh) + (dott(xh[kk * 128:, :K], rl) + dott(xl[kk * 128:, :K], rh)))
                g_ref[:, :128] = c[:128]
                col[kk * 128 + 128:, :] = c[128:]
        g_ref[:, 128:] = jnp.where(lane == row, 1.0, 0.0)
        for s in range(128 // SB):
            substep(g_ref, u_ref, s)
        k128 = pl.multiple_of(k * 128, 128)
        l_ref[pl.ds(k128, 128), pl.ds(k128, 128)] = jnp.where(lane <= row, u_ref[:, :128].T, 0.0)
        wh, wl = split(u_ref[:, 128:])
        for kk in range(n):
            @pl.when(k == kk)
            def _():
                ch, cl = split(col[kk * 128 + 128:, :])
                x = dott(ch, wh) + (dott(ch, wl) + dott(cl, wh))
                if kk < n - 1:
                    l_ref[kk * 128 + 128:, kk * 128:(kk + 1) * 128] = x[:1024 - kk * 128 - 128]
                    l_ref[:kk * 128 + 128, (kk + 1) * 128:(kk + 2) * 128] = jnp.zeros((kk * 128 + 128, 128), jnp.float32)
                x_ref[:, kk * 128:(kk + 1) * 128] = x[1024 - kk * 128 - 128:]
                h, l = split(x)
                xh[kk * 128 + 128:, kk * 128:(kk + 1) * 128] = h
                xl[kk * 128 + 128:, kk * 128:(kk + 1) * 128] = l
        return 0
    lax.fori_loop(0, n, step, 0)

def factor_panel(a, b):
    m = b.shape[0]
    vm = pl.BlockSpec(memory_space=pltpu.VMEM)
    return pl.pallas_call(
        functools.partial(kernel, m),
        out_shape=(jax.ShapeDtypeStruct((1024, 1024), jnp.float32), jax.ShapeDtypeStruct((m, 1024), jnp.float32)),
        in_specs=[vm, vm], out_specs=(vm, vm),
        scratch_shapes=[pltpu.VMEM((1024 + m, 1024), jnp.bfloat16), pltpu.VMEM((1024 + m, 1024), jnp.bfloat16),
                        pltpu.VMEM((1024 + m, 128), jnp.float32), pltpu.VMEM((128, 256), jnp.float32), pltpu.VMEM((128, 256), jnp.float32)],
        compiler_params=pltpu.CompilerParams(vmem_limit_bytes=60 * 2**20),
        name="factor_panel",
    )(a, b)


MESH = pl.DeviceIdType.MESH
NB = 8


class Place:
    def __init__(self, height):
        self.height = height
        self.m = BLK >> height
        self.leaf = lax.axis_index("leaf")
        self.f = lax.axis_index("front")
        self.core = lax.rem(self.leaf, 2)
        member = lax.rem(self.leaf, 2**height)
        piece = 0
        for bit in range(height):
            piece = piece + lax.rem(member // 2**bit, 2) * 2 ** (height - 1 - bit)
        self.piece = piece
        self.rest = lax.rem(piece, 2 ** (height - 1))
        self.peers = [self.flip(2 * d) for d in range(1, 2 ** (height - 1))]
        self.mate = self.flip(1)
        self.right = (self.leaf, lax.rem(self.f + 1, NB))
        self.left = (self.leaf, lax.rem(self.f + NB - 1, NB))

    def flip(self, mask):
        other = self.leaf
        bit = 1
        while bit <= mask:
            if mask & bit:
                other = other + bit * (1 - 2 * lax.rem(self.leaf // bit, 2))
            bit *= 2
        return (other, self.f)

    def greet(self):
        barrier = pltpu.get_barrier_semaphore()
        others = [self.left, self.right, self.mate] + self.peers
        for other in others:
            pl.semaphore_signal(barrier, inc=1, device_id=other, device_id_type=MESH)
        pl.semaphore_wait(barrier, len(others))


def guarded(cond, body):
    if cond is None:
        body()
    else:
        pl.when(cond)(body)


def remote(src, dst, send, recv, device):
    return pltpu.make_async_remote_copy(
        src_ref=src, dst_ref=dst, send_sem=send, recv_sem=recv, device_id=device, device_id_type=MESH
    )


GATHER_SEMS = [
    pltpu.SemaphoreType.DMA((3, NB)),
    pltpu.SemaphoreType.DMA((3, NB)),
    pltpu.SemaphoreType.DMA((2, 4, NB)),
    pltpu.SemaphoreType.DMA((2, 4, NB)),
    pltpu.SemaphoreType.DMA((NB, NB)),
    pltpu.SemaphoreType.DMA((NB, NB)),
]


def gather(place, whole, sems, lower):
    xs, xr, zs, zr, cs, cr = sems
    m = place.m

    def need(origin, q):
        return (origin >= q) if lower and q else None

    def slab(origin, q, core):
        return whole.at[origin, pl.ds(pl.multiple_of(core * 64, 64), 64), pl.ds(q * BLK, BLK)]

    def piece(index, q):
        rows = pl.ds(pl.multiple_of(index * m, m), m)
        return whole.at[place.f, rows, pl.ds(q * BLK, BLK)]

    def peer_copy(d, q):
        mine = piece(place.piece, q)
        return remote(mine, mine, xs.at[d, q], xr.at[d, q], place.peers[d])

    def ring_copy(way, hop, q):
        origin = lax.rem(place.f + ((NB - hop) if way == 0 else hop), NB)
        mine = slab(origin, q, place.core)
        return origin, remote(mine, mine, zs.at[way, hop, q], zr.at[way, hop, q], (place.right, place.left)[way])

    def arrival(way, hop, q):
        origin = lax.rem(place.f + ((NB - hop) if way == 0 else hop), NB)
        mine = slab(origin, q, place.core)
        return origin, remote(mine, mine, zs.at[way, hop - 1, q], zr.at[way, hop - 1, q], (place.right, place.left)[way])

    def mate_copy(origin, slot, q):
        mine = slab(origin, q, place.core)
        return remote(mine, mine, cs.at[slot, q], cr.at[slot, q], place.mate)

    def hops(way, q):
        return 4 if q % 2 == way else 3

    for q in range(NB):
        for d in range(len(place.peers)):
            guarded(need(place.f, q), lambda: peer_copy(d, q).start())
    for q in range(NB):
        def own():
            for d in range(len(place.peers)):
                peer_copy(d, q).wait_recv()
            for way in range(2):
                ring_copy(way, 0, q)[1].start()
            mate_copy(place.f, 0, q).start()
        guarded(need(place.f, q), own)
    for hop in range(1, 5):
        for q in range(NB):
            for way in range(2):
                if hop > hops(way, q):
                    continue
                origin, copy = arrival(way, hop, q)
                slot = hop if way == 0 else NB - hop
                def take():
                    copy.wait_recv()
                    if hop < hops(way, q):
                        ring_copy(way, hop, q)[1].start()
                    mate_copy(origin, slot, q).start()
                guarded(need(origin, q), take)
    for slot in range(NB):
        origin = lax.rem(place.f + NB - slot, NB)
        for q in range(NB):
            def close():
                copy = mate_copy(origin, slot, q)
                copy.wait_send()
                copy.wait_recv()
            guarded(need(origin, q), close)
    for q in range(NB):
        for way in range(2):
            for hop in range(hops(way, q)):
                origin, copy = ring_copy(way, hop, q)
                guarded(need(origin, q), lambda: copy.wait_send())
        for d in range(len(place.peers)):
            guarded(need(place.f, q), lambda: peer_copy(d, q).wait_send())


def assemble_kernel(height, update, entries, routes, whole, low, high, got, ex, *sems):
    place = Place(height)
    m = place.m
    bit = lax.rem(place.leaf // 2 ** (height - 1), 2)
    sibling = place.flip(2 ** (height - 1))
    place.greet()
    out_rows = pl.ds(pl.multiple_of((1 - bit) * m, m), m)
    own_rows = pl.ds(pl.multiple_of(bit * m, m), m)
    swap = remote(update.at[out_rows], got, ex.at[0], ex.at[1], sibling)
    swap.start()
    front = place.leaf // 2**height

    def upper(child, j):
        return jnp.where(routes[front, child, j] >= NB, 1.0, 0.0)

    mine = pl.ds(pl.multiple_of(place.piece * m, m), m)
    row_own = upper(bit, place.f)
    row_other = upper(1 - bit, place.f)
    for j in range(NB):
        cols = pl.ds(j * BLK, BLK)
        kept = update[own_rows, cols]
        up = upper(bit, j)
        whole[place.f, mine, cols] = entries[:m, cols] + ((1.0 - row_own) * (1.0 - up)) * kept
        low[:, cols] = entries[m:, cols] + (row_own * (1.0 - up)) * kept
        high[:, cols] = (row_own * up) * kept
    swap.wait()
    for j in range(NB):
        cols = pl.ds(j * BLK, BLK)
        other = got[:, cols]
        up = upper(1 - bit, j)
        whole[place.f, mine, cols] = whole[place.f, mine, cols] + ((1.0 - row_other) * (1.0 - up)) * other
        low[:, cols] = low[:, cols] + (row_other * (1.0 - up)) * other
        high[:, cols] = high[:, cols] + (row_other * up) * other
    gather(place, whole, sems, True)


def assemble_gather(height, update, entries, routes):
    m = BLK >> height
    vm = pl.BlockSpec(memory_space=pltpu.VMEM)
    sm = pl.BlockSpec(memory_space=pltpu.SMEM)
    f32 = jnp.float32
    return pl.pallas_call(
        functools.partial(assemble_kernel, height),
        out_shape=(
            jax.ShapeDtypeStruct((NB, BLK, 1024), f32),
            jax.ShapeDtypeStruct((m, 1024), f32),
            jax.ShapeDtypeStruct((m, 1024), f32),
        ),
        in_specs=[vm, vm, sm],
        out_specs=(vm, vm, vm),
        scratch_shapes=[pltpu.VMEM((m, 1024), f32), pltpu.SemaphoreType.DMA((2,))] + GATHER_SEMS,
        compiler_params=pltpu.CompilerParams(collective_id=2 * height, has_side_effects=True, vmem_limit_bytes=40 * 2**20),
        name="assemble_gather",
    )(update, entries, routes)


def schur_kernel(height, panel, high, out, whole, own, *sems):
    place = Place(height)
    m = place.m
    place.greet()
    mine = pl.ds(pl.multiple_of(place.piece * m, m), m)
    for q in range(NB):
        whole[place.f, mine, pl.ds(q * BLK, BLK)] = panel[:, q * BLK : (q + 1) * BLK]
    gather(place, whole, sems, False)
    ph, plo = split(panel[...])
    for j in range(NB):
        xh, xl = split(whole[j])
        upd = dott(ph, xh) + (dott(ph, xl) + dott(plo, xh))
        out[:, j * BLK : (j + 1) * BLK] = high[:, j * BLK : (j + 1) * BLK] - upd


def schur_gather(height, panel, high):
    m = BLK >> height
    vm = pl.BlockSpec(memory_space=pltpu.VMEM)
    f32 = jnp.float32
    return pl.pallas_call(
        functools.partial(schur_kernel, height),
        out_shape=jax.ShapeDtypeStruct((m, 1024), f32),
        in_specs=[vm, vm],
        out_specs=vm,
        scratch_shapes=[pltpu.VMEM((NB, BLK, 1024), f32), pltpu.VMEM((8, 128), f32)] + GATHER_SEMS,
        compiler_params=pltpu.CompilerParams(collective_id=2 * height + 1, has_side_effects=True, vmem_limit_bytes=40 * 2**20),
        name="schur_gather",
    )(panel, high)


def own_rows(height, lower_factor):
    place = Place(height)
    start = place.f * BLK + place.piece * place.m
    return lax.dynamic_slice_in_dim(lower_factor, start, place.m, 0)


def local(
    leaf_contrib,
    entries_lower,
    entries_middle,
    entries_upper,
    assembly_lower,
    assembly_middle,
    assembly_upper,
):
    update = leaf_contrib
    results = []
    for height, entries, routes in (
        (1, entries_lower, assembly_lower),
        (2, entries_middle, assembly_middle),
        (3, entries_upper, assembly_upper),
    ):
        whole, low, high = assemble_gather(height, update, entries, routes)
        lower_factor, panel = factor_panel(whole.reshape(1024, 1024), low)
        update = schur_gather(height, panel, high)
        results.append(jnp.concatenate([own_rows(height, lower_factor), panel], axis=0))
    return (results[0], results[1], results[2], update)


def solution(mesh):
    in_specs = (
        P(("leaf", "front"), None),
        P(("leaf", "front"), None),
        P(("leaf", "front"), None),
        P(("leaf", "front"), None),
        P(),
        P(),
        P(),
    )
    out_specs = (
        P(("leaf", "front"), None),
        P(("leaf", "front"), None),
        P(("leaf", "front"), None),
        P(("leaf", "front"), None),
    )
    return jax.shard_map(local, mesh=mesh, in_specs=in_specs, out_specs=out_specs, check_vma=False)
```

```python
import functools

import jax
import jax.numpy as jnp
from jax import lax
from jax.experimental import pallas as pl
from jax.experimental.pallas import tpu as pltpu
from jax.sharding import PartitionSpec as P

BLK = 128
SB = 16

def split(x):
    h = x.astype(jnp.bfloat16)
    return h, (x - h.astype(jnp.float32)).astype(jnp.bfloat16)

def dotb(a, b):
    return jnp.dot(a, b, preferred_element_type=jnp.float32)

def dott(a, b):
    return lax.dot_general(a, b, (((1,), (1,)), ((), ())), preferred_element_type=jnp.float32)

def substep(g_ref, u_ref, s):
    base = s * SB
    p = g_ref[base:base + SB, :]
    cols = [jnp.broadcast_to(p[:, base + k:base + k + 1], (SB, 128)) for k in range(SB)]
    pl_, pr_ = p[:, :128], p[:, 128:]
    sub = lax.broadcasted_iota(jnp.int32, (SB, 128), 0)
    ul = jnp.zeros((SB, 128), jnp.float32)
    ur = jnp.zeros((SB, 128), jnp.float32)
    for r in range(SB):
        hit = sub == r
        v = cols[r]
        piv = jnp.broadcast_to(v[r:r + 1], (SB, 128))
        rs = lax.rsqrt(piv)
        inv = rs * rs
        rl = jnp.broadcast_to(pl_[r:r + 1], (SB, 128))
        rr = jnp.broadcast_to(pr_[r:r + 1], (SB, 128))
        ul = jnp.where(hit, rl * rs, ul)
        ur = jnp.where(hit, rr * rs, ur)
        vi = jnp.where(hit, 0.0, v * inv)
        for k in range(r + 1, SB):
            c = jnp.broadcast_to(cols[k][r:r + 1], (SB, 128))
            cols[k] = jnp.where(hit, c * inv, cols[k] - vi * c)
        pl_ = jnp.where(hit, rl * inv, pl_ - vi * rl)
        pr_ = jnp.where(hit, rr * inv, pr_ - vi * rr)
    u_ref[base:base + SB, :128] = ul
    u_ref[base:base + SB, 128:] = ur
    if s < 128 // SB - 1:
        lo = base + SB
        R = jnp.concatenate([pl_, pr_], 1)
        rh, rlo = split(R)
        parts = []
        def pad(x):
            z = []
            if base: z.append(jnp.zeros((base, 256), jnp.bfloat16))
            z.append(x)
            if 128 - lo: z.append(jnp.zeros((128 - lo, 256), jnp.bfloat16))
            return jnp.concatenate(z, 0)
        d = g_ref[lo:, :128]
        dh, dl = split(d)
        upd = dotb(jnp.concatenate([dh, dl], 1), jnp.concatenate([pad(rh), pad(rh)], 0)) + dotb(dh, pad(rlo))
        g_ref[lo:, :] = g_ref[lo:, :] - upd


MESH = pl.DeviceIdType.MESH
NB = 8


class Place:
    def __init__(self, height):
        self.m = BLK >> height
        self.leaf = lax.axis_index("leaf")
        self.f = lax.axis_index("front")
        self.core = lax.rem(self.leaf, 2)
        member = lax.rem(self.leaf, 2**height)
        piece = 0
        for bit in range(height):
            piece = piece + lax.rem(member // 2**bit, 2) * 2 ** (height - 1 - bit)
        self.piece = piece
        self.peers = [self.flip(2 * d) for d in range(1, 2 ** (height - 1))]
        self.mate = self.flip(1)
        self.right = (self.leaf, lax.rem(self.f + 1, NB))
        self.left = (self.leaf, lax.rem(self.f + NB - 1, NB))

    def flip(self, mask):
        other = self.leaf
        bit = 1
        while bit <= mask:
            if mask & bit:
                other = other + bit * (1 - 2 * lax.rem(self.leaf // bit, 2))
            bit *= 2
        return (other, self.f)

    def greet(self):
        barrier = pltpu.get_barrier_semaphore()
        others = [self.left, self.right, self.mate] + self.peers
        for other in others:
            pl.semaphore_signal(barrier, inc=1, device_id=other, device_id_type=MESH)
        pl.semaphore_wait(barrier, len(others))

    def before(self, hop, way):
        return lax.rem(self.f + ((NB - hop) if way == 0 else hop), NB)


def guarded(conds, body):
    live = [c for c in conds if c is not True]
    if any(c is False for c in live):
        return
    if not live:
        body()
        return
    both = live[0]
    for c in live[1:]:
        both = jnp.logical_and(both, c)
    pl.when(both)(body)


def remote(src, dst, send, recv, device):
    return pltpu.make_async_remote_copy(
        src_ref=src, dst_ref=dst, send_sem=send, recv_sem=recv, device_id=device, device_id_type=MESH
    )


GATHER_SEMS = [
    pltpu.SemaphoreType.DMA((3, NB)),
    pltpu.SemaphoreType.DMA((3, NB)),
    pltpu.SemaphoreType.DMA((2, 4, NB)),
    pltpu.SemaphoreType.DMA((2, 4, NB)),
    pltpu.SemaphoreType.DMA((NB, NB)),
    pltpu.SemaphoreType.DMA((NB, NB)),
]


class Gather:
    def __init__(self, place, buf, sems, lower):
        self.place, self.buf, self.sems, self.lower = place, buf, sems, lower

    def need(self, origin, q):
        if not self.lower or (isinstance(q, int) and q == 0):
            return True
        return origin >= q

    def slab(self, origin, q):
        start = pl.multiple_of(origin * BLK + self.place.core * 64, 64)
        return self.buf.at[q, pl.ds(start, 64), :]

    def peer_copy(self, d, q):
        p = self.place
        mine = self.buf.at[q, pl.ds(pl.multiple_of(p.f * BLK + p.piece * p.m, p.m), p.m), :]
        return remote(mine, mine, self.sems[0].at[d, q], self.sems[1].at[d, q], p.peers[d])

    def ring_copy(self, way, hop, q, origin):
        p = self.place
        mine = self.slab(origin, q)
        return remote(mine, mine, self.sems[2].at[way, hop, q], self.sems[3].at[way, hop, q], (p.right, p.left)[way])

    def mate_copy(self, origin, slot, q):
        mine = self.slab(origin, q)
        return remote(mine, mine, self.sems[4].at[slot, q], self.sems[5].at[slot, q], self.place.mate)

    def post(self, q, *conds):
        def body():
            for d in range(len(self.place.peers)):
                self.peer_copy(d, q).start()
        if self.place.peers:
            guarded([self.need(self.place.f, q), *conds], body)

    def begin(self, q, *conds):
        def body():
            for d in range(len(self.place.peers)):
                self.peer_copy(d, q).wait_recv()
            for way in range(2):
                self.ring_copy(way, 0, q, self.place.f).start()
            self.mate_copy(self.place.f, 0, q).start()
        guarded([self.need(self.place.f, q), *conds], body)

    def last(self, way, q):
        return q % 2 == way if isinstance(q, int) else lax.rem(q, 2) == way

    def hop(self, h, q, *conds):
        for way in range(2):
            origin = self.place.before(h, way)
            slot = h if way == 0 else NB - h
            def body():
                self.ring_copy(way, h - 1, q, origin).wait_recv()
                if h < 3:
                    self.ring_copy(way, h, q, origin).start()
                elif h == 3:
                    guarded([self.last(way, q)], lambda: self.ring_copy(way, 3, q, origin).start())
                self.mate_copy(origin, slot, q).start()
            guarded([self.need(origin, q), self.last(way, q) if h == 4 else True, *conds], body)

    def land(self, q):
        for slot in range(NB):
            origin = self.place.before(slot, 0)
            guarded([self.need(origin, q)], lambda: self.mate_copy(origin, slot, q).wait_recv())

    def close(self):
        def each(q, _):
            for slot in range(NB):
                origin = self.place.before(slot, 0)
                guarded([self.need(origin, q)], lambda: self.mate_copy(origin, slot, q).wait_send())
            for way in range(2):
                for h in range(4):
                    origin = self.place.before(h, way)
                    guarded(
                        [self.need(origin, q), self.last(way, q) if h == 3 else True],
                        lambda: self.ring_copy(way, h, q, origin).wait_send(),
                    )
            def peers():
                for d in range(len(self.place.peers)):
                    self.peer_copy(d, q).wait_send()
            if self.place.peers:
                guarded([self.need(self.place.f, q)], peers)
            return 0
        lax.fori_loop(0, NB, each, 0)


def level_kernel(height, update, entries, routes, fac, out, whole, pan, low, got, xh, xl, col, g_ref, u_ref, ex, *sems):
    place = Place(height)
    m = place.m
    f = place.f
    bit = lax.rem(place.leaf // 2 ** (height - 1), 2)
    sibling = place.flip(2 ** (height - 1))
    place.greet()
    out_rows = pl.ds(pl.multiple_of((1 - bit) * m, m), m)
    own_rows = pl.ds(pl.multiple_of(bit * m, m), m)
    swap = remote(update.at[out_rows], got, ex.at[0], ex.at[1], sibling)
    swap.start()
    front = place.leaf // 2**height

    def upper(child, j):
        return jnp.where(routes[front, child, j] >= NB, 1.0, 0.0)

    mine = pl.ds(pl.multiple_of(f * BLK + place.piece * m, m), m)
    row_own = upper(bit, f)
    row_other = upper(1 - bit, f)
    for j in range(NB):
        cols = pl.ds(j * BLK, BLK)
        kept = update[own_rows, cols]
        up = upper(bit, j)
        col[j * m : (j + 1) * m, :] = entries[:m, cols] + ((1.0 - row_own) * (1.0 - up)) * kept
        low[:, cols] = entries[m:, cols] + (row_own * (1.0 - up)) * kept
        out[:, cols] = (row_own * up) * kept
    fac[:m, :] = jnp.zeros((m, 1024), jnp.float32)
    swap.wait()
    for j in range(NB):
        other = got[:, j * BLK : (j + 1) * BLK]
        up = upper(1 - bit, j)
        whole[j, mine, :] = col[j * m : (j + 1) * m, :] + ((1.0 - row_other) * (1.0 - up)) * other
    pivots = Gather(place, whole, sems[:6], True)
    panels = Gather(place, pan, sems[6:], False)
    for q in range(NB):
        pivots.post(q)
    for j in range(NB):
        cols = pl.ds(j * BLK, BLK)
        other = got[:, cols]
        up = upper(1 - bit, j)
        low[:, cols] = low[:, cols] + (row_other * (1.0 - up)) * other
        out[:, cols] = out[:, cols] + (row_other * up) * other

    def wave(w):
        for h in range(4, -1, -1):
            q = w - h
            if 0 <= q < NB:
                if h:
                    pivots.hop(h, q)
                else:
                    pivots.begin(q)

    for w in range(5):
        wave(w)

    lane = lax.broadcasted_iota(jnp.int32, (BLK, BLK), 1)
    row = lax.broadcasted_iota(jnp.int32, (BLK, BLK), 0)

    def accumulate(q):
        panels.land(q)
        ph, plo = split(fac[m:, pl.ds(pl.multiple_of(q * BLK, BLK), BLK)])
        th, tl = split(pan[q])
        out[...] = out[...] - (dott(ph, th) + (dott(ph, tl) + dott(plo, th)))

    waves = {1: 5, 4: 6, 7: 7, 10: 8, 13: 9, 16: 10, 19: 11}
    first = 1 if height == 1 else 2

    def slot(k, s):
        for t, w in waves.items():
            if t % 8 == s:
                pl.when(k == t // 8)(lambda: wave(w))
        if s == 0:
            panels.post(k - 1, k >= 1)
            panels.hop(2, k - 2, k >= 2)
        if s == first:
            panels.begin(k - 1, k >= 1)
        if s == 5:
            panels.hop(1, k - 1, k >= 1)
        if s == 3:
            panels.hop(3, k - 2, k >= 2)
        if s == 6:
            panels.hop(4, k - 2, k >= 2)
        if s == 7:
            pl.when(k >= 3)(lambda: accumulate(k - 3))

    def step(k, _):
        pivots.land(k)
        for kk in range(NB):
            @pl.when(k == kk)
            def _():
                c = jnp.concatenate([whole[kk, kk * BLK :, :], low[:, kk * BLK : (kk + 1) * BLK]], 0)
                if kk:
                    K = kk * BLK
                    rh, rl = xh[K : K + BLK, :K], xl[K : K + BLK, :K]
                    c = c - (dott(xh[K:, :K], rh) + (dott(xh[K:, :K], rl) + dott(xl[K:, :K], rh)))
                g_ref[:, :BLK] = c[:BLK]
                col[kk * BLK + BLK :, :] = c[BLK:]
        g_ref[:, BLK:] = jnp.where(lane == row, 1.0, 0.0)
        for s in range(BLK // SB):
            substep(g_ref, u_ref, s)
            slot(k, s)
        col[pl.ds(pl.multiple_of(k * BLK, BLK), BLK), :] = jnp.where(lane <= row, u_ref[:, :BLK].T, 0.0)
        wh, wl = split(u_ref[:, BLK:])
        for kk in range(NB):
            @pl.when(k == kk)
            def _():
                K = kk * BLK
                ch, cl = split(col[K + BLK :, :])
                x = dott(ch, wh) + (dott(ch, wl) + dott(cl, wh))
                if kk < NB - 1:
                    col[K + BLK : 1024, :] = x[: 1024 - K - BLK]
                tail = x[1024 - K - BLK :]
                fac[m:, K : K + BLK] = tail
                pan[kk, mine, :] = tail
                h, l = split(x)
                xh[K + BLK :, K : K + BLK] = h
                xl[K + BLK :, K : K + BLK] = l

        @pl.when(f >= k)
        def _():
            fac[:m, pl.ds(pl.multiple_of(k * BLK, BLK), BLK)] = col[mine, :]

        return 0

    lax.fori_loop(0, NB, step, 0)
    panels.post(7)
    panels.hop(2, 6)
    accumulate(5)
    panels.begin(7)
    panels.hop(3, 6)
    panels.hop(1, 7)
    panels.hop(4, 6)
    panels.hop(2, 7)
    panels.hop(3, 7)
    accumulate(6)
    panels.hop(4, 7)
    accumulate(7)
    pivots.close()
    panels.close()


def level(height, update, entries, routes):
    m = BLK >> height
    vm = pl.BlockSpec(memory_space=pltpu.VMEM)
    sm = pl.BlockSpec(memory_space=pltpu.SMEM)
    f32, bf16 = jnp.float32, jnp.bfloat16
    return pl.pallas_call(
        functools.partial(level_kernel, height),
        out_shape=(jax.ShapeDtypeStruct((2 * m, 1024), f32), jax.ShapeDtypeStruct((m, 1024), f32)),
        in_specs=[vm, vm, sm],
        out_specs=(vm, vm),
        scratch_shapes=[
            pltpu.VMEM((NB, 1024, BLK), f32),
            pltpu.VMEM((NB, 1024, BLK), f32),
            pltpu.VMEM((m, 1024), f32),
            pltpu.VMEM((m, 1024), f32),
            pltpu.VMEM((1024 + m, 1024), bf16),
            pltpu.VMEM((1024 + m, 1024), bf16),
            pltpu.VMEM((1024 + m, BLK), f32),
            pltpu.VMEM((BLK, 2 * BLK), f32),
            pltpu.VMEM((BLK, 2 * BLK), f32),
            pltpu.SemaphoreType.DMA((2,)),
        ]
        + GATHER_SEMS
        + GATHER_SEMS,
        compiler_params=pltpu.CompilerParams(
            collective_id=height, has_side_effects=True, vmem_limit_bytes=48 * 2**20
        ),
        name="front_level",
    )(update, entries, routes)


def local(
    leaf_contrib,
    entries_lower,
    entries_middle,
    entries_upper,
    assembly_lower,
    assembly_middle,
    assembly_upper,
):
    lower, update = level(1, leaf_contrib, entries_lower, assembly_lower)
    middle, update = level(2, update, entries_middle, assembly_middle)
    upper, update = level(3, update, entries_upper, assembly_upper)
    return (lower, middle, upper, update)


def solution(mesh):
    in_specs = (
        P(("leaf", "front"), None),
        P(("leaf", "front"), None),
        P(("leaf", "front"), None),
        P(("leaf", "front"), None),
        P(),
        P(),
        P(),
    )
    out_specs = (
        P(("leaf", "front"), None),
        P(("leaf", "front"), None),
        P(("leaf", "front"), None),
        P(("leaf", "front"), None),
    )
    return jax.shard_map(local, mesh=mesh, in_specs=in_specs, out_specs=out_specs, check_vma=False)
```

```python
import functools

import jax
import jax.numpy as jnp
from jax import lax
from jax.experimental import pallas as pl
from jax.experimental.pallas import tpu as pltpu
from jax.sharding import PartitionSpec as P

BLK = 128
SB = 16

def split(x):
    h = x.astype(jnp.bfloat16)
    return h, (x - h.astype(jnp.float32)).astype(jnp.bfloat16)

def dotb(a, b):
    return jnp.dot(a, b, preferred_element_type=jnp.float32)

def dott(a, b):
    return lax.dot_general(a, b, (((1,), (1,)), ((), ())), preferred_element_type=jnp.float32)

def substep(g_ref, u_ref, s):
    base = s * SB
    p = g_ref[base:base + SB, :]
    cols = [jnp.broadcast_to(p[:, base + k:base + k + 1], (SB, 128)) for k in range(SB)]
    pl_, pr_ = p[:, :128], p[:, 128:]
    sub = lax.broadcasted_iota(jnp.int32, (SB, 128), 0)
    ul = jnp.zeros((SB, 128), jnp.float32)
    ur = jnp.zeros((SB, 128), jnp.float32)
    for r in range(SB):
        hit = sub == r
        v = cols[r]
        piv = jnp.broadcast_to(v[r:r + 1], (SB, 128))
        rs = lax.rsqrt(piv)
        inv = rs * rs
        rl = jnp.broadcast_to(pl_[r:r + 1], (SB, 128))
        rr = jnp.broadcast_to(pr_[r:r + 1], (SB, 128))
        ul = jnp.where(hit, rl * rs, ul)
        ur = jnp.where(hit, rr * rs, ur)
        vi = jnp.where(hit, 0.0, v * inv)
        for k in range(r + 1, SB):
            c = jnp.broadcast_to(cols[k][r:r + 1], (SB, 128))
            cols[k] = jnp.where(hit, c * inv, cols[k] - vi * c)
        pl_ = jnp.where(hit, rl * inv, pl_ - vi * rl)
        pr_ = jnp.where(hit, rr * inv, pr_ - vi * rr)
    u_ref[base:base + SB, :128] = ul
    u_ref[base:base + SB, 128:] = ur
    lo = base + SB
    if lo < 128:
        near = g_ref[lo:lo + SB, :]
        sums = [near[:, :128], near[:, 128:]]
        parts = [None, None]
        for k in range(SB):
            dk = jnp.broadcast_to(near[:, base + k:base + k + 1], (SB, 128))
            tl = dk * jnp.broadcast_to(pl_[k:k + 1], (SB, 128))
            tr = dk * jnp.broadcast_to(pr_[k:k + 1], (SB, 128))
            if k % 2:
                sums = [sums[0] - tl, sums[1] - tr]
            else:
                parts = [tl, tr] if parts[0] is None else [parts[0] + tl, parts[1] + tr]
        g_ref[lo:lo + SB, :128] = sums[0] - parts[0]
        g_ref[lo:lo + SB, 128:] = sums[1] - parts[1]
    hi = lo + SB
    if hi < 128:
        rh, rlo = split(jnp.concatenate([pl_, pr_], 1))
        def pad(x):
            z = [jnp.zeros((base, 256), jnp.bfloat16)] if base else []
            return jnp.concatenate(z + [x, jnp.zeros((128 - lo, 256), jnp.bfloat16)], 0)
        dh, dl = split(g_ref[hi:, :128])
        ph = pad(rh)
        upd = dotb(jnp.concatenate([dh, dl], 1), jnp.concatenate([ph, ph], 0)) + dotb(dh, pad(rlo))
        g_ref[hi:, :] = g_ref[hi:, :] - upd


MESH = pl.DeviceIdType.MESH
NB = 8


class Place:
    def __init__(self, height):
        self.m = BLK >> height
        self.leaf = lax.axis_index("leaf")
        self.f = lax.axis_index("front")
        self.core = lax.rem(self.leaf, 2)
        member = lax.rem(self.leaf, 2**height)
        piece = 0
        for bit in range(height):
            piece = piece + lax.rem(member // 2**bit, 2) * 2 ** (height - 1 - bit)
        self.piece = piece
        self.peers = [self.flip(2 * d) for d in range(1, 2 ** (height - 1))]
        self.mate = self.flip(1)

    def flip(self, mask):
        other = self.leaf
        bit = 1
        while bit <= mask:
            if mask & bit:
                other = other + bit * (1 - 2 * lax.rem(self.leaf // bit, 2))
            bit *= 2
        return (other, self.f)

    def greet(self):
        barrier = pltpu.get_barrier_semaphore()
        others = [(self.leaf, lax.rem(self.f + d, NB)) for d in range(1, NB)] + [self.mate] + self.peers
        for other in others:
            pl.semaphore_signal(barrier, inc=1, device_id=other, device_id_type=MESH)
        pl.semaphore_wait(barrier, len(others))


def guarded(conds, body):
    live = [c for c in conds if c is not True]
    if any(c is False for c in live):
        return
    if not live:
        body()
        return
    both = live[0]
    for c in live[1:]:
        both = jnp.logical_and(both, c)
    pl.when(both)(body)


def remote(src, dst, send, recv, device):
    return pltpu.make_async_remote_copy(
        src_ref=src, dst_ref=dst, send_sem=send, recv_sem=recv, device_id=device, device_id_type=MESH
    )


GATHER_SEMS = [pltpu.SemaphoreType.DMA((NB,)) for _ in range(10)]


class Gather:
    def __init__(self, place, buf, sems, lower):
        self.place, self.buf, self.sems, self.lower = place, buf, sems, lower

    def low(self, q):
        return q if self.lower else 0

    def mine(self):
        p = self.place
        return pl.ds(pl.multiple_of(p.piece * p.m, p.m), p.m)

    def half(self):
        return pl.ds(pl.multiple_of(self.place.core * 64, 64), 64)

    def blocks(self, q, rows, count=None):
        lo = self.low(q)
        return self.buf.at[q, pl.ds(lo, NB - lo if count is None else count), rows, :]

    def ring_copy(self, step, q):
        p = self.place
        own = self.buf.at[q, pl.ds(p.f, 1), self.mine(), :]
        to = (p.leaf, lax.rem(p.f + step, NB))
        return remote(own, own, self.sems[0].at[q], self.sems[1].at[q], to)

    def peer_copy(self, d, q):
        own = self.blocks(q, self.mine())
        return remote(own, own, self.sems[2 + d].at[q], self.sems[5].at[q], self.place.peers[d])

    def mate_copy(self, q):
        own = self.blocks(q, self.half())
        return remote(own, own, self.sems[6].at[q], self.sems[7].at[q], self.place.mate)

    def all_of(self, q, sem, count):
        rows = self.buf.at[q, pl.ds(0, count), self.mine(), :]
        return remote(rows, rows, sem, sem, self.place.mate)

    def counted(self, q, sem, count, most, sending):
        def wait(n):
            copy = self.all_of(q, sem, n)
            copy.wait_send() if sending else copy.wait_recv()
        if isinstance(count, int):
            wait(count)
            return
        for n in range(1, most + 1):
            pl.when(count == n)(lambda: wait(n))

    def has(self, origin, q):
        return 1 if self.low(q) == 0 else jnp.where(origin >= q, 1, 0)

    def at(self, step):
        return lax.rem(self.place.f + step, NB)

    def relay_copy(self, origin, step, q):
        own = self.buf.at[q, pl.ds(origin, 1), self.mine(), :]
        return remote(own, own, self.sems[8].at[q], self.sems[9].at[q], (self.place.leaf, self.at(step)))

    def odd(self, q):
        return q % 2 if isinstance(q, int) else lax.rem(q, 2)

    def relay(self, q, *conds):
        def body():
            self.counted(q, self.sems[1].at[q], self.has(self.at(6), q) + self.has(self.at(2), q), 2, False)
            for back, far, parity in ((6, 2, 0), (2, 6, 1)):
                origin = self.at(back)
                def pair():
                    self.relay_copy(origin, 1, q).start()
                    self.relay_copy(origin, 7, q).start()
                    odd = self.odd(q)
                    guarded([odd == parity], lambda: self.relay_copy(origin, far, q).start())
                guarded([True if self.low(q) == 0 else origin >= q], pair)
        guarded([*conds], body)

    def relayed(self, q):
        total = 0
        for step in (1, 3, 4, 5, 7):
            total = total + self.has(self.at(step), q)
        return total

    def relays(self, q):
        left, right = self.has(self.at(6), q), self.has(self.at(2), q)
        return 2 * left + 2 * right + (right if q % 2 else left)

    def holds(self, q):
        return True if self.low(q) == 0 else self.place.f >= q

    def send(self, q, *conds, tree=False):
        def body():
            for step in (2, 6) if tree else (4, 3, 5, 2, 6, 1, 7):
                self.ring_copy(step, q).start()
        guarded([self.holds(q), *conds], body)

    def spread(self, q, *conds, tree=False):
        def body():
            if tree:
                self.counted(q, self.sems[9].at[q], self.relayed(q), 5, False)
            elif self.low(q) == 0:
                self.counted(q, self.sems[1].at[q], NB - 1, 7, False)
            else:
                self.counted(q, self.sems[1].at[q], NB - q - self.has(self.place.f, q), NB - q, False)
            for d in range(len(self.place.peers)):
                self.peer_copy(d, q).start()
            if not self.place.peers:
                self.mate_copy(q).start()
        guarded([*conds], body)

    def cross(self, q, *conds):
        n = len(self.place.peers)
        def body():
            if n == 1:
                self.peer_copy(0, q).wait_recv()
            else:
                lo = self.low(q)
                rows = self.blocks(q, pl.ds(0, n * self.place.m))
                remote(rows, rows, self.sems[5].at[q], self.sems[5].at[q], self.place.mate).wait_recv()
            self.mate_copy(q).start()
        if n:
            guarded([*conds], body)

    def land(self, q):
        self.mate_copy(q).wait_recv()

    def close(self, trees):
        for q in range(NB):
            count = 2 if q in trees else NB - 1
            guarded([self.holds(q)], lambda: self.all_of(q, self.sems[0].at[q], count).wait_send())
            if q in trees:
                self.counted(q, self.sems[8].at[q], self.relays(q), 5, True)
            for d in range(len(self.place.peers)):
                self.peer_copy(d, q).wait_send()
            self.mate_copy(q).wait_send()


def level_kernel(height, update, entries, routes, fac, out, whole, pan, low, got, xh, xl, col, g_ref, u_ref, ex, *sems):
    place = Place(height)
    m = place.m
    f = place.f
    bit = lax.rem(place.leaf // 2 ** (height - 1), 2)
    sibling = place.flip(2 ** (height - 1))
    place.greet()
    out_rows = pl.ds(pl.multiple_of((1 - bit) * m, m), m)
    own_rows = pl.ds(pl.multiple_of(bit * m, m), m)
    swap = remote(update.at[out_rows], got, ex.at[0], ex.at[1], sibling)
    swap.start()
    front = place.leaf // 2**height

    def upper(child, j):
        return jnp.where(routes[front, child, j] >= NB, 1.0, 0.0)

    mine = pl.ds(pl.multiple_of(place.piece * m, m), m)
    row_own = upper(bit, f)
    row_other = upper(1 - bit, f)
    for j in range(NB):
        cols = pl.ds(j * BLK, BLK)
        kept = update[own_rows, cols]
        up = upper(bit, j)
        col[j * m : (j + 1) * m, :] = entries[:m, cols] + ((1.0 - row_own) * (1.0 - up)) * kept
        low[:, cols] = entries[m:, cols] + (row_own * (1.0 - up)) * kept
        out[:, cols] = (row_own * up) * kept
    fac[:m, :] = jnp.zeros((m, 1024), jnp.float32)
    swap.wait()
    for j in range(NB):
        other = got[:, j * BLK : (j + 1) * BLK]
        up = upper(1 - bit, j)
        whole[j, f, mine, :] = col[j * m : (j + 1) * m, :] + ((1.0 - row_other) * (1.0 - up)) * other
    pivots = Gather(place, whole, sems[:10], True)
    panels = Gather(place, pan, sems[10:], False)
    pivots.send(0)
    pivots.send(1)
    for j in range(NB):
        cols = pl.ds(j * BLK, BLK)
        other = got[:, cols]
        up = upper(1 - bit, j)
        low[:, cols] = low[:, cols] + (row_other * (1.0 - up)) * other
        out[:, cols] = out[:, cols] + (row_other * up) * other

    pair = height == 1
    pivot_trees = range(2, NB) if pair else ()
    panel_trees = range(4) if pair else ()
    pivots.spread(0)
    pivots.send(2, tree=pair)
    if not pair:
        pivots.spread(1)
        pivots.cross(0)

    lane = lax.broadcasted_iota(jnp.int32, (BLK, BLK), 1)
    row = lax.broadcasted_iota(jnp.int32, (BLK, BLK), 0)

    def accumulate(q):
        panels.land(q)
        ph, plo = split(fac[m:, pl.ds(pl.multiple_of(q * BLK, BLK), BLK)])
        th, tl = split(pan[q].reshape(1024, BLK))
        out[...] = out[...] - (dott(ph, th) + (dott(ph, tl) + dott(plo, th)))

    plan = {}

    def at(k, half, name, q):
        plan.setdefault((k, half), []).append((name, q))

    if pair:
        at(0, 0, "spread", 1)
        at(0, 1, "relay", 2)
        at(1, 0, "spread", 2)
        for q in range(3, NB):
            at(q - 3, 0, "send", q)
            at(q - 2, 0, "relay", q)
            at(q - 1, 0, "spread", q)
    else:
        at(0, 1, "cross", 1)
        at(0, 1, "spread", 2)
        at(1, 1, "cross", 2)
        for q in range(3, NB):
            at(q - 3, 0, "send", q)
            at(q - 2, 1, "spread", q)
            at(q - 1, 1, "cross", q)

    def slot(k, half):
        for (kk, hh), acts in plan.items():
            if hh == half:
                def go():
                    for name, q in acts:
                        if name in ("send", "spread"):
                            getattr(pivots, name)(q, tree=q in pivot_trees)
                        else:
                            getattr(pivots, name)(q)
                pl.when(k == kk)(go)
        split_at = len(panel_trees)
        if half == 0:
            if pair:
                panels.send(k - 1, k >= 1, k - 1 < split_at, tree=True)
            panels.send(k - 1, k >= 1, k - 1 >= split_at)
            if pair:
                panels.relay(k - 2, k >= 2, k - 2 < split_at)
                panels.spread(k - 3, k >= 3, k - 3 >= split_at)
            pl.when(k >= 4)(lambda: accumulate(k - 4))
        elif pair:
            panels.spread(k - 3, k >= 3, k - 3 < split_at, tree=True)
        else:
            panels.spread(k - 2, k >= 2)
            panels.cross(k - 3, k >= 3)

    def step(k, _):
        for kk in range(NB):
            @pl.when(k == kk)
            def _():
                pivots.land(kk)
                block = whole[kk, kk:, :, :].reshape((NB - kk) * BLK, BLK)
                c = jnp.concatenate([block, low[:, kk * BLK : (kk + 1) * BLK]], 0)
                if kk:
                    K = kk * BLK
                    rh, rl = xh[K : K + BLK, :K], xl[K : K + BLK, :K]
                    c = c - (dott(xh[K:, :K], rh) + (dott(xh[K:, :K], rl) + dott(xl[K:, :K], rh)))
                g_ref[:, :BLK] = c[:BLK]
                col[kk * BLK + BLK :, :] = c[BLK:]
        g_ref[:, BLK:] = jnp.where(lane == row, 1.0, 0.0)
        slot(k, 0)
        for s in range(BLK // SB):
            substep(g_ref, u_ref, s)
            if s == 3:
                slot(k, 1)
        col[pl.ds(pl.multiple_of(k * BLK, BLK), BLK), :] = jnp.where(lane <= row, u_ref[:, :BLK].T, 0.0)
        wh, wl = split(u_ref[:, BLK:])
        for kk in range(NB):
            @pl.when(k == kk)
            def _():
                K = kk * BLK
                ch, cl = split(col[K + BLK :, :])
                x = dott(ch, wh) + (dott(ch, wl) + dott(cl, wh))
                if kk < NB - 1:
                    col[K + BLK : 1024, :] = x[: 1024 - K - BLK]
                tail = x[1024 - K - BLK :]
                fac[m:, K : K + BLK] = tail
                pan[kk, f, mine, :] = tail
                h, l = split(x)
                xh[K + BLK :, K : K + BLK] = h
                xl[K + BLK :, K : K + BLK] = l

        @pl.when(f >= k)
        def _():
            fac[:m, pl.ds(pl.multiple_of(k * BLK, BLK), BLK)] = col[pl.ds(pl.multiple_of(f * BLK + place.piece * m, m), m), :]

        return 0

    lax.fori_loop(0, NB, step, 0)
    panels.send(7)
    accumulate(4)
    if pair:
        panels.spread(5)
        panels.spread(6)
        accumulate(5)
        panels.spread(7)
    else:
        panels.spread(6)
        panels.cross(5)
        accumulate(5)
        panels.spread(7)
        panels.cross(6)
    accumulate(6)
    panels.cross(7)
    accumulate(7)
    pivots.close(pivot_trees)
    panels.close(panel_trees)


def level(height, update, entries, routes):
    m = BLK >> height
    vm = pl.BlockSpec(memory_space=pltpu.VMEM)
    sm = pl.BlockSpec(memory_space=pltpu.SMEM)
    f32, bf16 = jnp.float32, jnp.bfloat16
    return pl.pallas_call(
        functools.partial(level_kernel, height),
        out_shape=(jax.ShapeDtypeStruct((2 * m, 1024), f32), jax.ShapeDtypeStruct((m, 1024), f32)),
        in_specs=[vm, vm, sm],
        out_specs=(vm, vm),
        scratch_shapes=[
            pltpu.VMEM((NB, NB, BLK, BLK), f32),
            pltpu.VMEM((NB, NB, BLK, BLK), f32),
            pltpu.VMEM((m, 1024), f32),
            pltpu.VMEM((m, 1024), f32),
            pltpu.VMEM((1024 + m, 1024), bf16),
            pltpu.VMEM((1024 + m, 1024), bf16),
            pltpu.VMEM((1024 + m, BLK), f32),
            pltpu.VMEM((BLK, 2 * BLK), f32),
            pltpu.VMEM((BLK, 2 * BLK), f32),
            pltpu.SemaphoreType.DMA((2,)),
        ]
        + GATHER_SEMS
        + GATHER_SEMS,
        compiler_params=pltpu.CompilerParams(
            collective_id=height, has_side_effects=True, vmem_limit_bytes=48 * 2**20
        ),
        name="front_level",
    )(update, entries, routes)


def local(
    leaf_contrib,
    entries_lower,
    entries_middle,
    entries_upper,
    assembly_lower,
    assembly_middle,
    assembly_upper,
):
    lower, update = level(1, leaf_contrib, entries_lower, assembly_lower)
    middle, update = level(2, update, entries_middle, assembly_middle)
    upper, update = level(3, update, entries_upper, assembly_upper)
    return (lower, middle, upper, update)


def solution(mesh):
    in_specs = (
        P(("leaf", "front"), None),
        P(("leaf", "front"), None),
        P(("leaf", "front"), None),
        P(("leaf", "front"), None),
        P(),
        P(),
        P(),
    )
    out_specs = (
        P(("leaf", "front"), None),
        P(("leaf", "front"), None),
        P(("leaf", "front"), None),
        P(("leaf", "front"), None),
    )
    return jax.shard_map(local, mesh=mesh, in_specs=in_specs, out_specs=out_specs, check_vma=False)
```

```python
import functools

import jax
import jax.numpy as jnp
from jax import lax
from jax.experimental import pallas as pl
from jax.experimental.pallas import tpu as pltpu
from jax.sharding import PartitionSpec as P

BLK = 128
SB = 16

def split(x):
    h = x.astype(jnp.bfloat16)
    return h, (x - h.astype(jnp.float32)).astype(jnp.bfloat16)

def dotb(a, b):
    return jnp.dot(a, b, preferred_element_type=jnp.float32)

def dott(a, b):
    return lax.dot_general(a, b, (((1,), (1,)), ((), ())), preferred_element_type=jnp.float32)

def substep(g_ref, u_ref, s):
    base = s * SB
    p = g_ref[base:base + SB, :]
    cols = [jnp.broadcast_to(p[:, base + k:base + k + 1], (SB, 128)) for k in range(SB)]
    pl_, pr_ = p[:, :128], p[:, 128:]
    sub = lax.broadcasted_iota(jnp.int32, (SB, 128), 0)
    ul = jnp.zeros((SB, 128), jnp.float32)
    ur = jnp.zeros((SB, 128), jnp.float32)
    for r in range(SB):
        hit = sub == r
        v = cols[r]
        piv = jnp.broadcast_to(v[r:r + 1], (SB, 128))
        rs = lax.rsqrt(piv)
        inv = rs * rs
        rl = jnp.broadcast_to(pl_[r:r + 1], (SB, 128))
        rr = jnp.broadcast_to(pr_[r:r + 1], (SB, 128))
        ul = jnp.where(hit, rl * rs, ul)
        ur = jnp.where(hit, rr * rs, ur)
        vi = jnp.where(hit, 0.0, v * inv)
        for k in range(r + 1, SB):
            c = jnp.broadcast_to(cols[k][r:r + 1], (SB, 128))
            cols[k] = jnp.where(hit, c * inv, cols[k] - vi * c)
        pl_ = jnp.where(hit, rl * inv, pl_ - vi * rl)
        pr_ = jnp.where(hit, rr * inv, pr_ - vi * rr)
    u_ref[base:base + SB, :128] = ul
    u_ref[base:base + SB, 128:] = ur
    lo = base + SB
    if lo < 128:
        near = g_ref[lo:lo + SB, :]
        sums = [near[:, :128], near[:, 128:]]
        parts = [None, None]
        for k in range(SB):
            dk = jnp.broadcast_to(near[:, base + k:base + k + 1], (SB, 128))
            tl = dk * jnp.broadcast_to(pl_[k:k + 1], (SB, 128))
            tr = dk * jnp.broadcast_to(pr_[k:k + 1], (SB, 128))
            if k % 2:
                sums = [sums[0] - tl, sums[1] - tr]
            else:
                parts = [tl, tr] if parts[0] is None else [parts[0] + tl, parts[1] + tr]
        g_ref[lo:lo + SB, :128] = sums[0] - parts[0]
        g_ref[lo:lo + SB, 128:] = sums[1] - parts[1]
    hi = lo + SB
    if hi < 128:
        rh, rlo = split(jnp.concatenate([pl_, pr_], 1))
        def pad(x):
            z = [jnp.zeros((base, 256), jnp.bfloat16)] if base else []
            return jnp.concatenate(z + [x, jnp.zeros((128 - lo, 256), jnp.bfloat16)], 0)
        dh, dl = split(g_ref[hi:, :128])
        ph = pad(rh)
        upd = dotb(jnp.concatenate([dh, dl], 1), jnp.concatenate([ph, ph], 0)) + dotb(dh, pad(rlo))
        g_ref[hi:, :] = g_ref[hi:, :] - upd


MESH = pl.DeviceIdType.MESH
NB = 8


class Place:
    def __init__(self, height):
        self.m = BLK >> height
        self.leaf = lax.axis_index("leaf")
        self.f = lax.axis_index("front")
        self.core = lax.rem(self.leaf, 2)
        member = lax.rem(self.leaf, 2**height)
        piece = 0
        for bit in range(height):
            piece = piece + lax.rem(member // 2**bit, 2) * 2 ** (height - 1 - bit)
        self.piece = piece
        self.peers = [self.flip(2 * d) for d in range(1, 2 ** (height - 1))]
        self.mate = self.flip(1)

    def flip(self, mask):
        other = self.leaf
        bit = 1
        while bit <= mask:
            if mask & bit:
                other = other + bit * (1 - 2 * lax.rem(self.leaf // bit, 2))
            bit *= 2
        return (other, self.f)

    def greet(self):
        barrier = pltpu.get_barrier_semaphore()
        others = [(self.leaf, lax.rem(self.f + d, NB)) for d in range(1, NB)] + [self.mate] + self.peers
        for other in others:
            pl.semaphore_signal(barrier, inc=1, device_id=other, device_id_type=MESH)
        n = len(self.peers)
        if n == 0:
            pl.semaphore_wait(barrier, len(others))
            return
        for leaf, _ in self.peers:
            @pl.when(self.f != 0)
            def _():
                pl.semaphore_signal(barrier, inc=1, device_id=(leaf, 0), device_id_type=MESH)
        @pl.when(self.f != 0)
        def _():
            pl.semaphore_wait(barrier, len(others))
        @pl.when(self.f == 0)
        def _():
            pl.semaphore_wait(barrier, len(others) + (NB - 1) * n)


def guarded(conds, body):
    live = [c for c in conds if c is not True]
    if any(c is False for c in live):
        return
    if not live:
        body()
        return
    both = live[0]
    for c in live[1:]:
        both = jnp.logical_and(both, c)
    pl.when(both)(body)


def remote(src, dst, send, recv, device):
    return pltpu.make_async_remote_copy(
        src_ref=src, dst_ref=dst, send_sem=send, recv_sem=recv, device_id=device, device_id_type=MESH
    )


GATHER_SEMS = [pltpu.SemaphoreType.DMA((NB,)) for _ in range(10)]


class Gather:
    def __init__(self, place, buf, sems, lower):
        self.place, self.buf, self.sems, self.lower = place, buf, sems, lower

    def low(self, q):
        return max(q, 1) if self.lower else 0

    def mine(self):
        p = self.place
        return pl.ds(pl.multiple_of(p.piece * p.m, p.m), p.m)

    def half(self):
        return pl.ds(pl.multiple_of(self.place.core * 64, 64), 64)

    def blocks(self, q, rows, count=None):
        lo = self.low(q)
        return self.buf.at[q, pl.ds(lo, NB - lo if count is None else count), rows, :]

    def ring_copy(self, step, q):
        p = self.place
        own = self.buf.at[q, pl.ds(p.f, 1), self.mine(), :]
        to = (p.leaf, lax.rem(p.f + step, NB))
        return remote(own, own, self.sems[0].at[q], self.sems[1].at[q], to)

    def peer_copy(self, d, q):
        own = self.blocks(q, self.mine())
        return remote(own, own, self.sems[2 + d].at[q], self.sems[5].at[q], self.place.peers[d])

    def mate_copy(self, q):
        own = self.blocks(q, self.half())
        return remote(own, own, self.sems[6].at[q], self.sems[7].at[q], self.place.mate)

    def all_of(self, q, sem, count):
        rows = self.buf.at[q, pl.ds(0, count), self.mine(), :]
        return remote(rows, rows, sem, sem, self.place.mate)

    def counted(self, q, sem, count, most, sending):
        def wait(n):
            copy = self.all_of(q, sem, n)
            copy.wait_send() if sending else copy.wait_recv()
        if isinstance(count, int):
            wait(count)
            return
        for n in range(1, most + 1):
            pl.when(count == n)(lambda: wait(n))

    def has(self, origin, q):
        return 1 if self.low(q) == 0 else jnp.where(origin >= self.low(q), 1, 0)

    def at(self, step):
        return lax.rem(self.place.f + step, NB)

    def relay_copy(self, origin, step, q):
        own = self.buf.at[q, pl.ds(origin, 1), self.mine(), :]
        return remote(own, own, self.sems[8].at[q], self.sems[9].at[q], (self.place.leaf, self.at(step)))

    def odd(self, q):
        return q % 2 if isinstance(q, int) else lax.rem(q, 2)

    def relay(self, q, *conds):
        def body():
            self.counted(q, self.sems[1].at[q], self.has(self.at(6), q) + self.has(self.at(2), q), 2, False)
            for back, far, parity in ((6, 2, 0), (2, 6, 1)):
                origin = self.at(back)
                def pair():
                    self.relay_copy(origin, 1, q).start()
                    self.relay_copy(origin, 7, q).start()
                    odd = self.odd(q)
                    guarded([odd == parity], lambda: self.relay_copy(origin, far, q).start())
                guarded([True if self.low(q) == 0 else origin >= self.low(q)], pair)
        guarded([*conds], body)

    def relayed(self, q):
        total = 0
        for step in (1, 3, 4, 5, 7):
            total = total + self.has(self.at(step), q)
        return total

    def relays(self, q):
        left, right = self.has(self.at(6), q), self.has(self.at(2), q)
        return 2 * left + 2 * right + (right if q % 2 else left)

    def holds(self, q):
        return True if self.low(q) == 0 else self.place.f >= self.low(q)

    def send(self, q, *conds, tree=False):
        def body():
            for step in (2, 6) if tree else (4, 3, 5, 2, 6, 1, 7):
                self.ring_copy(step, q).start()
        guarded([self.holds(q), *conds], body)

    def spread(self, q, *conds, tree=False):
        def body():
            if tree:
                self.counted(q, self.sems[9].at[q], self.relayed(q), 5, False)
            elif self.low(q) == 0:
                self.counted(q, self.sems[1].at[q], NB - 1, 7, False)
            else:
                self.counted(q, self.sems[1].at[q], NB - self.low(q) - self.has(self.place.f, q), NB - self.low(q), False)
            for d in range(len(self.place.peers)):
                self.peer_copy(d, q).start()
            if not self.place.peers:
                self.mate_copy(q).start()
        guarded([*conds], body)

    def cross(self, q, *conds):
        n = len(self.place.peers)
        def body():
            if n == 1:
                self.peer_copy(0, q).wait_recv()
            else:
                lo = self.low(q)
                rows = self.blocks(q, pl.ds(0, n * self.place.m))
                remote(rows, rows, self.sems[5].at[q], self.sems[5].at[q], self.place.mate).wait_recv()
            self.mate_copy(q).start()
        if n:
            guarded([*conds], body)

    def land(self, q):
        self.mate_copy(q).wait_recv()

    def close(self, trees):
        for q in range(NB):
            count = 2 if q in trees else NB - 1
            guarded([self.holds(q)], lambda: self.all_of(q, self.sems[0].at[q], count).wait_send())
            if q in trees:
                self.counted(q, self.sems[8].at[q], self.relays(q), 5, True)
            for d in range(len(self.place.peers)):
                self.peer_copy(d, q).wait_send()
            self.mate_copy(q).wait_send()


class Seed:
    def __init__(self, place, buf, sems):
        self.place, self.sems, self.block = place, sems, buf.at[0, 0]
        self.owner = place.f == 0
        self.mine = self.block.at[pl.ds(pl.multiple_of(place.piece * place.m, place.m), place.m), :]

    def sized(self, count, send, recv):
        rows = self.block.at[pl.ds(0, count), :]
        return remote(rows, rows, send, recv, self.place.mate)

    def send(self):
        p = self.place
        def body():
            for step in (4, 3, 5, 2, 6, 1, 7):
                for leaf in [p.leaf] + [peer[0] for peer in p.peers]:
                    to = (leaf, lax.rem(p.f + step, NB))
                    remote(self.mine, self.mine, self.sems.at[0], self.sems.at[2], to).start()
            for peer in p.peers:
                remote(self.mine, self.mine, self.sems.at[1], self.sems.at[2], peer).start()
        pl.when(self.owner)(body)

    def forward(self):
        p = self.place
        n = len(p.peers)
        sem = self.sems.at[2]
        if n:
            pl.when(self.owner)(lambda: self.sized(n * p.m, sem, sem).wait_recv())
        pl.when(jnp.logical_not(self.owner))(lambda: self.sized(64, sem, sem).wait_recv())
        self.mate_copy().start()

    def mate_copy(self):
        half = self.block.at[pl.ds(pl.multiple_of(self.place.core * 64, 64), 64), :]
        return remote(half, half, self.sems.at[3], self.sems.at[4], self.place.mate)

    def land(self):
        self.mate_copy().wait_recv()

    def close(self, buf):
        p = self.place
        def body():
            rows = buf.at[0, pl.ds(0, NB - 1), pl.ds(0, 64), :]
            remote(rows, rows, self.sems.at[0], self.sems.at[0], p.mate).wait_send()
            if p.peers:
                self.sized(len(p.peers) * p.m, self.sems.at[1], self.sems.at[1]).wait_send()
        pl.when(self.owner)(body)
        self.mate_copy().wait_send()


def level_kernel(height, update, entries, routes, fac, out, whole, pan, low, got, xh, xl, col, g_ref, u_ref, ex, early, *sems):
    place = Place(height)
    m = place.m
    f = place.f
    bit = lax.rem(place.leaf // 2 ** (height - 1), 2)
    sibling = place.flip(2 ** (height - 1))
    place.greet()
    out_rows = pl.ds(pl.multiple_of((1 - bit) * m, m), m)
    own_rows = pl.ds(pl.multiple_of(bit * m, m), m)
    swap = remote(update.at[out_rows], got, ex.at[0], ex.at[1], sibling)
    swap.start()
    front = place.leaf // 2**height

    def upper(child, j):
        return jnp.where(routes[front, child, j] >= NB, 1.0, 0.0)

    mine = pl.ds(pl.multiple_of(place.piece * m, m), m)
    row_own = upper(bit, f)
    row_other = upper(1 - bit, f)
    for j in range(NB):
        cols = pl.ds(j * BLK, BLK)
        kept = update[own_rows, cols]
        up = upper(bit, j)
        col[j * m : (j + 1) * m, :] = entries[:m, cols] + ((1.0 - row_own) * (1.0 - up)) * kept
        low[:, cols] = entries[m:, cols] + (row_own * (1.0 - up)) * kept
        out[:, cols] = (row_own * up) * kept
    fac[:m, :] = jnp.zeros((m, 1024), jnp.float32)
    swap.wait()
    for j in range(NB):
        other = got[:, j * BLK : (j + 1) * BLK]
        up = upper(1 - bit, j)
        whole[j, f, mine, :] = col[j * m : (j + 1) * m, :] + ((1.0 - row_other) * (1.0 - up)) * other
    pivots = Gather(place, whole, sems[:10], True)
    panels = Gather(place, pan, sems[10:], False)
    seed = Seed(place, whole, early)
    seed.send()
    pivots.send(0)
    pivots.send(1)
    for j in range(NB):
        cols = pl.ds(j * BLK, BLK)
        other = got[:, cols]
        up = upper(1 - bit, j)
        low[:, cols] = low[:, cols] + (row_other * (1.0 - up)) * other
        out[:, cols] = out[:, cols] + (row_other * up) * other

    pair = height == 1
    pivot_trees = range(2, NB) if pair else ()
    panel_trees = range(4) if pair else ()
    pair = height == 1
    pivot_trees = range(2, NB) if pair else ()
    panel_trees = range(6) if pair else ()
    seed.forward()
    if not pair:
        pivots.spread(0)
        pivots.send(2)
    seed.land()

    lane = lax.broadcasted_iota(jnp.int32, (BLK, BLK), 1)
    row = lax.broadcasted_iota(jnp.int32, (BLK, BLK), 0)

    def accumulate(q):
        panels.land(q)
        ph, plo = split(fac[m:, pl.ds(pl.multiple_of(q * BLK, BLK), BLK)])
        th, tl = split(pan[q].reshape(1024, BLK))
        out[...] = out[...] - (dott(ph, th) + (dott(ph, tl) + dott(plo, th)))

    plan = {}

    def at(k, half, name, q):
        plan.setdefault((k, half), []).append((name, q))

    if pair:
        at(0, 1, "spread", 0)
        at(0, 1, "send", 2)
        at(0, 2, "spread", 1)
        at(1, 0, "relay", 2)
        at(1, 2, "spread", 2)
        for q in range(3, NB):
            at(q - 3, 1, "send", q)
            at(q - 2, 1, "relay", q)
            at(q - 1, 1, "spread", q)
    else:
        at(0, 0, "spread", 1)
        at(0, 1, "cross", 0)
        at(0, 2, "cross", 1)
        at(0, 2, "spread", 2)
        at(1, 1, "cross", 2)
        for q in range(3, NB):
            at(q - 3, 1, "send", q)
            at(q - 2, 1, "spread", q)
            at(q - 1, 1, "cross", q)

    def slot(k, half):
        for (kk, hh), acts in plan.items():
            if hh == half:
                def go():
                    for name, q in acts:
                        if name in ("send", "spread"):
                            getattr(pivots, name)(q, tree=q in pivot_trees)
                        else:
                            getattr(pivots, name)(q)
                pl.when(k == kk)(go)
        split_at = len(panel_trees)
        if half == 0:
            if pair:
                panels.send(k - 1, k >= 1, k - 1 < split_at, tree=True)
            panels.send(k - 1, k >= 1, k - 1 >= split_at)
            if pair:
                panels.relay(k - 2, k >= 2, k - 2 < split_at)
            pl.when(k >= 4)(lambda: accumulate(k - 4))
        elif half == 1 and pair:
            panels.spread(k - 3, k >= 3, k - 3 < split_at, tree=True)
        elif half == 1:
            panels.spread(k - 2, k >= 2)
            panels.cross(k - 3, k >= 3)

    def step(k, _):
        for kk in range(NB):
            @pl.when(k == kk)
            def _():
                if kk == 0:
                    g_ref[:, :BLK] = whole[0, 0]
                    return
                pivots.land(kk)
                block = whole[kk, kk:, :, :].reshape((NB - kk) * BLK, BLK)
                c = jnp.concatenate([block, low[:, kk * BLK : (kk + 1) * BLK]], 0)
                if kk:
                    K = kk * BLK
                    rh, rl = xh[K : K + BLK, :K], xl[K : K + BLK, :K]
                    c = c - (dott(xh[K:, :K], rh) + (dott(xh[K:, :K], rl) + dott(xl[K:, :K], rh)))
                g_ref[:, :BLK] = c[:BLK]
                col[kk * BLK + BLK :, :] = c[BLK:]
        g_ref[:, BLK:] = jnp.where(lane == row, 1.0, 0.0)
        slot(k, 0)
        for s in range(BLK // SB):
            substep(g_ref, u_ref, s)
            if s == 3:
                slot(k, 1)
        slot(k, 2)
        col[pl.ds(pl.multiple_of(k * BLK, BLK), BLK), :] = jnp.where(lane <= row, u_ref[:, :BLK].T, 0.0)
        wh, wl = split(u_ref[:, BLK:])
        for kk in range(NB):
            @pl.when(k == kk)
            def _():
                K = kk * BLK
                if kk == 0:
                    pivots.land(0)
                    col[BLK:1024, :] = whole[0, 1:].reshape(1024 - BLK, BLK)
                    col[1024:, :] = low[:, :BLK]
                ch, cl = split(col[K + BLK :, :])
                x = dott(ch, wh) + (dott(ch, wl) + dott(cl, wh))
                if kk < NB - 1:
                    col[K + BLK : 1024, :] = x[: 1024 - K - BLK]
                tail = x[1024 - K - BLK :]
                fac[m:, K : K + BLK] = tail
                pan[kk, f, mine, :] = tail
                h, l = split(x)
                xh[K + BLK :, K : K + BLK] = h
                xl[K + BLK :, K : K + BLK] = l

        @pl.when(f >= k)
        def _():
            fac[:m, pl.ds(pl.multiple_of(k * BLK, BLK), BLK)] = col[pl.ds(pl.multiple_of(f * BLK + place.piece * m, m), m), :]

        return 0

    lax.fori_loop(0, NB, step, 0)
    panels.send(7)
    accumulate(4)
    if pair:
        panels.spread(5, tree=True)
        panels.spread(6)
        accumulate(5)
        panels.spread(7)
    else:
        panels.spread(6)
        panels.cross(5)
        accumulate(5)
        panels.spread(7)
        panels.cross(6)
    accumulate(6)
    panels.cross(7)
    accumulate(7)
    seed.close(whole)
    pivots.close(pivot_trees)
    panels.close(panel_trees)


def level(height, update, entries, routes):
    m = BLK >> height
    vm = pl.BlockSpec(memory_space=pltpu.VMEM)
    sm = pl.BlockSpec(memory_space=pltpu.SMEM)
    f32, bf16 = jnp.float32, jnp.bfloat16
    return pl.pallas_call(
        functools.partial(level_kernel, height),
        out_shape=(jax.ShapeDtypeStruct((2 * m, 1024), f32), jax.ShapeDtypeStruct((m, 1024), f32)),
        in_specs=[vm, vm, sm],
        out_specs=(vm, vm),
        scratch_shapes=[
            pltpu.VMEM((NB, NB, BLK, BLK), f32),
            pltpu.VMEM((NB, NB, BLK, BLK), f32),
            pltpu.VMEM((m, 1024), f32),
            pltpu.VMEM((m, 1024), f32),
            pltpu.VMEM((1024 + m, 1024), bf16),
            pltpu.VMEM((1024 + m, 1024), bf16),
            pltpu.VMEM((1024 + m, BLK), f32),
            pltpu.VMEM((BLK, 2 * BLK), f32),
            pltpu.VMEM((BLK, 2 * BLK), f32),
            pltpu.SemaphoreType.DMA((2,)),
            pltpu.SemaphoreType.DMA((5,)),
        ]
        + GATHER_SEMS
        + GATHER_SEMS,
        compiler_params=pltpu.CompilerParams(
            collective_id=height, has_side_effects=True, vmem_limit_bytes=48 * 2**20
        ),
        name="front_level",
    )(update, entries, routes)


def local(
    leaf_contrib,
    entries_lower,
    entries_middle,
    entries_upper,
    assembly_lower,
    assembly_middle,
    assembly_upper,
):
    lower, update = level(1, leaf_contrib, entries_lower, assembly_lower)
    middle, update = level(2, update, entries_middle, assembly_middle)
    upper, update = level(3, update, entries_upper, assembly_upper)
    return (lower, middle, upper, update)


def solution(mesh):
    in_specs = (
        P(("leaf", "front"), None),
        P(("leaf", "front"), None),
        P(("leaf", "front"), None),
        P(("leaf", "front"), None),
        P(),
        P(),
        P(),
    )
    out_specs = (
        P(("leaf", "front"), None),
        P(("leaf", "front"), None),
        P(("leaf", "front"), None),
        P(("leaf", "front"), None),
    )
    return jax.shard_map(local, mesh=mesh, in_specs=in_specs, out_specs=out_specs, check_vma=False)
```

```python
import functools

import jax
import jax.numpy as jnp
from jax import lax
from jax.experimental import pallas as pl
from jax.experimental.pallas import tpu as pltpu
from jax.sharding import PartitionSpec as P

BLK = 128
SB = 16

def split(x):
    h = x.astype(jnp.bfloat16)
    return h, (x - h.astype(jnp.float32)).astype(jnp.bfloat16)

def dotb(a, b):
    return jnp.dot(a, b, preferred_element_type=jnp.float32)

def dott(a, b):
    return lax.dot_general(a, b, (((1,), (1,)), ((), ())), preferred_element_type=jnp.float32)

def substep(g_ref, u_ref, s):
    base = s * SB
    p = g_ref[base:base + SB, :]
    cols = [jnp.broadcast_to(p[:, base + k:base + k + 1], (SB, 128)) for k in range(SB)]
    pl_, pr_ = p[:, :128], p[:, 128:]
    sub = lax.broadcasted_iota(jnp.int32, (SB, 128), 0)
    ul = jnp.zeros((SB, 128), jnp.float32)
    ur = jnp.zeros((SB, 128), jnp.float32)
    for r in range(SB):
        hit = sub == r
        v = cols[r]
        piv = jnp.broadcast_to(v[r:r + 1], (SB, 128))
        rs = lax.rsqrt(piv)
        inv = rs * rs
        rl = jnp.broadcast_to(pl_[r:r + 1], (SB, 128))
        rr = jnp.broadcast_to(pr_[r:r + 1], (SB, 128))
        ul = jnp.where(hit, rl * rs, ul)
        ur = jnp.where(hit, rr * rs, ur)
        vi = jnp.where(hit, 0.0, v * inv)
        for k in range(r + 1, SB):
            c = jnp.broadcast_to(cols[k][r:r + 1], (SB, 128))
            cols[k] = jnp.where(hit, c * inv, cols[k] - vi * c)
        pl_ = jnp.where(hit, rl * inv, pl_ - vi * rl)
        pr_ = jnp.where(hit, rr * inv, pr_ - vi * rr)
    u_ref[base:base + SB, :128] = ul
    u_ref[base:base + SB, 128:] = ur
    lo = base + SB
    if lo < 128:
        near = g_ref[lo:lo + SB, :]
        sums = [near[:, :128], near[:, 128:]]
        parts = [None, None]
        for k in range(SB):
            dk = jnp.broadcast_to(near[:, base + k:base + k + 1], (SB, 128))
            tl = dk * jnp.broadcast_to(pl_[k:k + 1], (SB, 128))
            tr = dk * jnp.broadcast_to(pr_[k:k + 1], (SB, 128))
            if k % 2:
                sums = [sums[0] - tl, sums[1] - tr]
            else:
                parts = [tl, tr] if parts[0] is None else [parts[0] + tl, parts[1] + tr]
        g_ref[lo:lo + SB, :128] = sums[0] - parts[0]
        g_ref[lo:lo + SB, 128:] = sums[1] - parts[1]
    hi = lo + SB
    if hi < 128:
        rh, rlo = split(jnp.concatenate([pl_, pr_], 1))
        def pad(x):
            z = [jnp.zeros((base, 256), jnp.bfloat16)] if base else []
            return jnp.concatenate(z + [x, jnp.zeros((128 - lo, 256), jnp.bfloat16)], 0)
        dh, dl = split(g_ref[hi:, :128])
        ph = pad(rh)
        upd = dotb(jnp.concatenate([dh, dl], 1), jnp.concatenate([ph, ph], 0)) + dotb(dh, pad(rlo))
        g_ref[hi:, :] = g_ref[hi:, :] - upd


MESH = pl.DeviceIdType.MESH
NB = 8


class Place:
    def __init__(self, height):
        self.m = BLK >> height
        self.leaf = lax.axis_index("leaf")
        self.f = lax.axis_index("front")
        self.core = lax.rem(self.leaf, 2)
        member = lax.rem(self.leaf, 2**height)
        piece = 0
        for bit in range(height):
            piece = piece + lax.rem(member // 2**bit, 2) * 2 ** (height - 1 - bit)
        self.piece = piece
        self.peers = [self.flip(2 * d) for d in range(1, 2 ** (height - 1))]
        self.mate = self.flip(1)

    def flip(self, mask):
        other = self.leaf
        bit = 1
        while bit <= mask:
            if mask & bit:
                other = other + bit * (1 - 2 * lax.rem(self.leaf // bit, 2))
            bit *= 2
        return (other, self.f)

    def greet(self):
        barrier = pltpu.get_barrier_semaphore()
        others = [(self.leaf, lax.rem(self.f + d, NB)) for d in range(1, NB)] + [self.mate] + self.peers
        for other in others:
            pl.semaphore_signal(barrier, inc=1, device_id=other, device_id_type=MESH)
        n = len(self.peers)
        if n == 0:
            pl.semaphore_wait(barrier, len(others))
            return
        for leaf, _ in self.peers:
            @pl.when(self.f != 0)
            def _():
                pl.semaphore_signal(barrier, inc=1, device_id=(leaf, 0), device_id_type=MESH)
        @pl.when(self.f != 0)
        def _():
            pl.semaphore_wait(barrier, len(others))
        @pl.when(self.f == 0)
        def _():
            pl.semaphore_wait(barrier, len(others) + (NB - 1) * n)


def guarded(conds, body):
    live = [c for c in conds if c is not True]
    if any(c is False for c in live):
        return
    if not live:
        body()
        return
    both = live[0]
    for c in live[1:]:
        both = jnp.logical_and(both, c)
    pl.when(both)(body)


def remote(src, dst, send, recv, device):
    return pltpu.make_async_remote_copy(
        src_ref=src, dst_ref=dst, send_sem=send, recv_sem=recv, device_id=device, device_id_type=MESH
    )


GATHER_SEMS = [pltpu.SemaphoreType.DMA((NB,)) for _ in range(10)]


class Gather:
    def __init__(self, place, buf, sems, lower):
        self.place, self.buf, self.sems, self.lower = place, buf, sems, lower

    def low(self, q):
        return max(q, 1) if self.lower else 0

    def mine(self):
        p = self.place
        return pl.ds(pl.multiple_of(p.piece * p.m, p.m), p.m)

    def half(self):
        return pl.ds(pl.multiple_of(self.place.core * 64, 64), 64)

    def blocks(self, q, rows, count=None):
        lo = self.low(q)
        return self.buf.at[q, pl.ds(lo, NB - lo if count is None else count), rows, :]

    def ring_copy(self, step, q):
        p = self.place
        own = self.buf.at[q, pl.ds(p.f, 1), self.mine(), :]
        to = (p.leaf, lax.rem(p.f + step, NB))
        return remote(own, own, self.sems[0].at[q], self.sems[1].at[q], to)

    def peer_copy(self, d, q):
        own = self.blocks(q, self.mine())
        return remote(own, own, self.sems[2 + d].at[q], self.sems[5].at[q], self.place.peers[d])

    def mate_copy(self, q):
        own = self.blocks(q, self.half())
        return remote(own, own, self.sems[6].at[q], self.sems[7].at[q], self.place.mate)

    def all_of(self, q, sem, count):
        rows = self.buf.at[q, pl.ds(0, count), self.mine(), :]
        return remote(rows, rows, sem, sem, self.place.mate)

    def counted(self, q, sem, count, most, sending):
        def wait(n):
            copy = self.all_of(q, sem, n)
            copy.wait_send() if sending else copy.wait_recv()
        if isinstance(count, int):
            wait(count)
            return
        for n in range(1, most + 1):
            pl.when(count == n)(lambda: wait(n))

    def has(self, origin, q):
        return 1 if self.low(q) == 0 else jnp.where(origin >= self.low(q), 1, 0)

    def at(self, step):
        return lax.rem(self.place.f + step, NB)

    def relay_copy(self, origin, step, q):
        own = self.buf.at[q, pl.ds(origin, 1), self.mine(), :]
        return remote(own, own, self.sems[8].at[q], self.sems[9].at[q], (self.place.leaf, self.at(step)))

    def odd(self, q):
        return q % 2 if isinstance(q, int) else lax.rem(q, 2)

    def relay(self, q, *conds):
        def body():
            self.counted(q, self.sems[1].at[q], self.has(self.at(6), q) + self.has(self.at(2), q), 2, False)
            for back, far, parity in ((6, 2, 0), (2, 6, 1)):
                origin = self.at(back)
                def pair():
                    self.relay_copy(origin, 1, q).start()
                    self.relay_copy(origin, 7, q).start()
                    odd = self.odd(q)
                    guarded([odd == parity], lambda: self.relay_copy(origin, far, q).start())
                guarded([True if self.low(q) == 0 else origin >= self.low(q)], pair)
        guarded([*conds], body)

    def relayed(self, q):
        total = 0
        for step in (1, 3, 4, 5, 7):
            total = total + self.has(self.at(step), q)
        return total

    def relays(self, q):
        left, right = self.has(self.at(6), q), self.has(self.at(2), q)
        return 2 * left + 2 * right + (right if q % 2 else left)

    def holds(self, q):
        return True if self.low(q) == 0 else self.place.f >= self.low(q)

    def send(self, q, *conds, tree=False):
        def body():
            for step in (2, 6) if tree else (4, 3, 5, 2, 6, 1, 7):
                self.ring_copy(step, q).start()
        guarded([self.holds(q), *conds], body)

    def spread(self, q, *conds, tree=False):
        def body():
            if tree:
                self.counted(q, self.sems[9].at[q], self.relayed(q), 5, False)
            elif self.low(q) == 0:
                self.counted(q, self.sems[1].at[q], NB - 1, 7, False)
            else:
                self.counted(q, self.sems[1].at[q], NB - self.low(q) - self.has(self.place.f, q), NB - self.low(q), False)
            for d in range(len(self.place.peers)):
                self.peer_copy(d, q).start()
            if not self.place.peers:
                self.mate_copy(q).start()
        guarded([*conds], body)

    def cross(self, q, *conds):
        n = len(self.place.peers)
        def body():
            if n == 1:
                self.peer_copy(0, q).wait_recv()
            else:
                lo = self.low(q)
                rows = self.blocks(q, pl.ds(0, n * self.place.m))
                remote(rows, rows, self.sems[5].at[q], self.sems[5].at[q], self.place.mate).wait_recv()
            self.mate_copy(q).start()
        if n:
            guarded([*conds], body)

    def land(self, q):
        self.mate_copy(q).wait_recv()

    def close(self, trees):
        for q in range(NB):
            count = 2 if q in trees else NB - 1
            guarded([self.holds(q)], lambda: self.all_of(q, self.sems[0].at[q], count).wait_send())
            if q in trees:
                self.counted(q, self.sems[8].at[q], self.relays(q), 5, True)
            for d in range(len(self.place.peers)):
                self.peer_copy(d, q).wait_send()
            self.mate_copy(q).wait_send()


class Seed:
    def __init__(self, place, buf, sems):
        self.place, self.sems, self.block = place, sems, buf.at[0, 0]
        self.owner = place.f == 0
        self.mine = self.block.at[pl.ds(pl.multiple_of(place.piece * place.m, place.m), place.m), :]

    def sized(self, count, send, recv):
        rows = self.block.at[pl.ds(0, count), :]
        return remote(rows, rows, send, recv, self.place.mate)

    def send(self):
        p = self.place
        def body():
            for step in (4, 3, 5, 2, 6, 1, 7):
                for leaf in [p.leaf] + [peer[0] for peer in p.peers]:
                    to = (leaf, lax.rem(p.f + step, NB))
                    remote(self.mine, self.mine, self.sems.at[0], self.sems.at[2], to).start()
            for peer in p.peers:
                remote(self.mine, self.mine, self.sems.at[1], self.sems.at[2], peer).start()
        pl.when(self.owner)(body)

    def forward(self):
        p = self.place
        n = len(p.peers)
        sem = self.sems.at[2]
        if n:
            pl.when(self.owner)(lambda: self.sized(n * p.m, sem, sem).wait_recv())
        pl.when(jnp.logical_not(self.owner))(lambda: self.sized(64, sem, sem).wait_recv())
        self.mate_copy().start()

    def mate_copy(self):
        half = self.block.at[pl.ds(pl.multiple_of(self.place.core * 64, 64), 64), :]
        return remote(half, half, self.sems.at[3], self.sems.at[4], self.place.mate)

    def land(self):
        self.mate_copy().wait_recv()

    def close(self, buf):
        p = self.place
        def body():
            rows = buf.at[0, pl.ds(0, NB - 1), pl.ds(0, 64), :]
            remote(rows, rows, self.sems.at[0], self.sems.at[0], p.mate).wait_send()
            if p.peers:
                self.sized(len(p.peers) * p.m, self.sems.at[1], self.sems.at[1]).wait_send()
        pl.when(self.owner)(body)
        self.mate_copy().wait_send()


def level_kernel(height, update, entries, routes, fac, out, whole, pan, low, got, xh, xl, col, g_ref, u_ref, ex, early, *sems):
    place = Place(height)
    m = place.m
    f = place.f
    bit = lax.rem(place.leaf // 2 ** (height - 1), 2)
    sibling = place.flip(2 ** (height - 1))
    place.greet()
    out_rows = pl.ds(pl.multiple_of((1 - bit) * m, m), m)
    own_rows = pl.ds(pl.multiple_of(bit * m, m), m)
    swap = remote(update.at[out_rows], got, ex.at[0], ex.at[1], sibling)
    swap.start()
    front = place.leaf // 2**height

    def upper(child, j):
        return jnp.where(routes[front, child, j] >= NB, 1.0, 0.0)

    mine = pl.ds(pl.multiple_of(place.piece * m, m), m)
    row_own = upper(bit, f)
    row_other = upper(1 - bit, f)
    for j in range(NB):
        cols = pl.ds(j * BLK, BLK)
        kept = update[own_rows, cols]
        up = upper(bit, j)
        col[j * m : (j + 1) * m, :] = entries[:m, cols] + ((1.0 - row_own) * (1.0 - up)) * kept
        low[:, cols] = entries[m:, cols] + (row_own * (1.0 - up)) * kept
        out[:, cols] = (row_own * up) * kept
    fac[:m, :] = jnp.zeros((m, 1024), jnp.float32)
    swap.wait()
    for j in range(NB):
        other = got[:, j * BLK : (j + 1) * BLK]
        up = upper(1 - bit, j)
        whole[j, f, mine, :] = col[j * m : (j + 1) * m, :] + ((1.0 - row_other) * (1.0 - up)) * other
    pivots = Gather(place, whole, sems[:10], True)
    panels = Gather(place, pan, sems[10:], False)
    seed = Seed(place, whole, early)
    seed.send()
    pivots.send(0)
    pivots.send(1)
    for j in range(NB):
        cols = pl.ds(j * BLK, BLK)
        other = got[:, cols]
        up = upper(1 - bit, j)
        low[:, cols] = low[:, cols] + (row_other * (1.0 - up)) * other
        out[:, cols] = out[:, cols] + (row_other * up) * other

    pair = height == 1
    pivot_trees = range(2, NB) if pair else ()
    panel_trees = range(4) if pair else ()
    pair = height == 1
    pivot_trees = range(2, NB) if pair else ()
    panel_trees = range(6) if pair else ()
    seed.forward()
    if not pair:
        pivots.spread(0)
        pivots.send(2)
    seed.land()

    lane = lax.broadcasted_iota(jnp.int32, (BLK, BLK), 1)
    row = lax.broadcasted_iota(jnp.int32, (BLK, BLK), 0)

    def accumulate(q):
        panels.land(q)
        ph, plo = split(fac[m:, pl.ds(pl.multiple_of(q * BLK, BLK), BLK)])
        th, tl = split(pan[q].reshape(1024, BLK))
        out[...] = out[...] - (dott(ph, th) + (dott(ph, tl) + dott(plo, th)))

    plan = {}

    def at(k, half, name, q):
        plan.setdefault((k, half), []).append((name, q))

    if pair:
        at(0, 1, "spread", 0)
        at(0, 1, "send", 2)
        at(0, 2, "spread", 1)
        at(1, 0, "relay", 2)
        at(1, 2, "spread", 2)
        for q in range(3, NB):
            at(q - 3, 1, "send", q)
            at(q - 2, 1, "relay", q)
            at(q - 1, 1, "spread", q)
    else:
        at(0, 0, "spread", 1)
        at(0, 1, "cross", 0)
        at(0, 2, "cross", 1)
        at(0, 2, "spread", 2)
        at(1, 1, "cross", 2)
        for q in range(3, NB):
            if height == 3:
                at(0, 0 if q < 5 else 1, "send", q)
                at(q - 2, 0, "spread", q)
            else:
                at(q - 3, 1, "send", q)
                at(q - 2, 1, "spread", q)
            at(q - 1, 1, "cross", q)

    def slot(k, half):
        for (kk, hh), acts in plan.items():
            if hh == half:
                def go():
                    for name, q in acts:
                        if name in ("send", "spread"):
                            getattr(pivots, name)(q, tree=q in pivot_trees)
                        else:
                            getattr(pivots, name)(q)
                pl.when(k == kk)(go)
        split_at = len(panel_trees)
        if half == 0:
            if pair:
                panels.send(k - 1, k >= 1, k - 1 < split_at, tree=True)
            panels.send(k - 1, k >= 1, k - 1 >= split_at)
            if pair:
                panels.relay(k - 2, k >= 2, k - 2 < split_at)
            pl.when(k >= 4)(lambda: accumulate(k - 4))
        elif half == 1 and pair:
            panels.spread(k - 3, k >= 3, k - 3 < split_at, tree=True)
        elif half == 1:
            panels.spread(k - 2, k >= 2)
            panels.cross(k - 3, k >= 3)

    def step(k, _):
        for kk in range(NB):
            @pl.when(k == kk)
            def _():
                if kk == 0:
                    g_ref[:, :BLK] = whole[0, 0]
                    return
                pivots.land(kk)
                block = whole[kk, kk:, :, :].reshape((NB - kk) * BLK, BLK)
                c = jnp.concatenate([block, low[:, kk * BLK : (kk + 1) * BLK]], 0)
                if kk:
                    K = kk * BLK
                    rh, rl = xh[K : K + BLK, :K], xl[K : K + BLK, :K]
                    c = c - (dott(xh[K:, :K], rh) + (dott(xh[K:, :K], rl) + dott(xl[K:, :K], rh)))
                g_ref[:, :BLK] = c[:BLK]
                col[kk * BLK + BLK :, :] = c[BLK:]
        g_ref[:, BLK:] = jnp.where(lane == row, 1.0, 0.0)
        slot(k, 0)
        for s in range(BLK // SB):
            substep(g_ref, u_ref, s)
            if s == 3:
                slot(k, 1)
        slot(k, 2)
        col[pl.ds(pl.multiple_of(k * BLK, BLK), BLK), :] = jnp.where(lane <= row, u_ref[:, :BLK].T, 0.0)
        wh, wl = split(u_ref[:, BLK:])
        for kk in range(NB):
            @pl.when(k == kk)
            def _():
                K = kk * BLK
                if kk == 0:
                    pivots.land(0)
                    col[BLK:1024, :] = whole[0, 1:].reshape(1024 - BLK, BLK)
                    col[1024:, :] = low[:, :BLK]
                ch, cl = split(col[K + BLK :, :])
                x = dott(ch, wh) + (dott(ch, wl) + dott(cl, wh))
                if kk < NB - 1:
                    col[K + BLK : 1024, :] = x[: 1024 - K - BLK]
                tail = x[1024 - K - BLK :]
                fac[m:, K : K + BLK] = tail
                pan[kk, f, mine, :] = tail
                h, l = split(x)
                xh[K + BLK :, K : K + BLK] = h
                xl[K + BLK :, K : K + BLK] = l

        @pl.when(f >= k)
        def _():
            fac[:m, pl.ds(pl.multiple_of(k * BLK, BLK), BLK)] = col[pl.ds(pl.multiple_of(f * BLK + place.piece * m, m), m), :]

        return 0

    lax.fori_loop(0, NB, step, 0)
    panels.send(7)
    accumulate(4)
    if pair:
        panels.spread(5, tree=True)
        panels.spread(6)
        accumulate(5)
        panels.spread(7)
    else:
        panels.spread(6)
        panels.cross(5)
        accumulate(5)
        panels.spread(7)
        panels.cross(6)
    accumulate(6)
    panels.cross(7)
    accumulate(7)
    seed.close(whole)
    pivots.close(pivot_trees)
    panels.close(panel_trees)


def level(height, update, entries, routes):
    m = BLK >> height
    vm = pl.BlockSpec(memory_space=pltpu.VMEM)
    sm = pl.BlockSpec(memory_space=pltpu.SMEM)
    f32, bf16 = jnp.float32, jnp.bfloat16
    return pl.pallas_call(
        functools.partial(level_kernel, height),
        out_shape=(jax.ShapeDtypeStruct((2 * m, 1024), f32), jax.ShapeDtypeStruct((m, 1024), f32)),
        in_specs=[vm, vm, sm],
        out_specs=(vm, vm),
        scratch_shapes=[
            pltpu.VMEM((NB, NB, BLK, BLK), f32),
            pltpu.VMEM((NB, NB, BLK, BLK), f32),
            pltpu.VMEM((m, 1024), f32),
            pltpu.VMEM((m, 1024), f32),
            pltpu.VMEM((1024 + m, 1024), bf16),
            pltpu.VMEM((1024 + m, 1024), bf16),
            pltpu.VMEM((1024 + m, BLK), f32),
            pltpu.VMEM((BLK, 2 * BLK), f32),
            pltpu.VMEM((BLK, 2 * BLK), f32),
            pltpu.SemaphoreType.DMA((2,)),
            pltpu.SemaphoreType.DMA((5,)),
        ]
        + GATHER_SEMS
        + GATHER_SEMS,
        compiler_params=pltpu.CompilerParams(
            collective_id=height, has_side_effects=True, vmem_limit_bytes=48 * 2**20
        ),
        name="front_level",
    )(update, entries, routes)


def local(
    leaf_contrib,
    entries_lower,
    entries_middle,
    entries_upper,
    assembly_lower,
    assembly_middle,
    assembly_upper,
):
    lower, update = level(1, leaf_contrib, entries_lower, assembly_lower)
    middle, update = level(2, update, entries_middle, assembly_middle)
    upper, update = level(3, update, entries_upper, assembly_upper)
    return (lower, middle, upper, update)


def solution(mesh):
    in_specs = (
        P(("leaf", "front"), None),
        P(("leaf", "front"), None),
        P(("leaf", "front"), None),
        P(("leaf", "front"), None),
        P(),
        P(),
        P(),
    )
    out_specs = (
        P(("leaf", "front"), None),
        P(("leaf", "front"), None),
        P(("leaf", "front"), None),
        P(("leaf", "front"), None),
    )
    return jax.shard_map(local, mesh=mesh, in_specs=in_specs, out_specs=out_specs, check_vma=False)
```
